32 devices in a mesh: pulse: 4 (over z), tile: 8 (over y, x, core).
Axes of the slice: x: 2, y: 2, z: 4, core: 2. Of those that a mesh axis runs over, the one named last changes fastest.
Arguments:
- echoes: bfloat16 [2, 128, 4, 16384], P(None, 'pulse', None, 'tile'), may hold values from -6 to 6
- replica: bfloat16 [2, 2048], replicated, may hold values from -0.09375 to 0.09375
- steer_phase: float32 [16, 16], replicated, may hold values from -3.140625 to 3.140625
- range_shift: int32 [2, 32], replicated, may hold values from -8 to 7
- merge_phase: float32 [2, 32], replicated, may hold values from -3.140625 to 3.140625
- merge_frac: float32 [2, 32], replicated, may hold values from 0 to 1
- footprint: int32 [4, 128], P('pulse', 'tile'), may hold values from 0 to 7, as said below
- row_slot: int32 [4, 128], P('pulse', 'tile'), may hold values from 0 to 15
- beam_index: int32 [4, 128, 128], P('pulse', 'tile'), may hold values from 0 to 30
- beam_frac: bfloat16 [4, 128, 128], P('pulse', 'tile'), may hold values from 0 to 1
Outputs:
- image: bfloat16 [2, 4, 128, 16384], P(None, None, 'pulse', 'tile')
The draws below stay inside these ranges and needn't reach their ends.
Inputs may be any that keep to these rules, and one draw needn't show every extreme that they name: `footprint`: of the 16 blocks of one tile and one pulse block, at most 2 fall on any one tile; in every draw one tile receives exactly 2 blocks from every tile and pulse block.
All inputs are finite; a program needn't handle non-finite values.
Results may differ from the reference program's by a relative error of at most 0.018.
Values may be sent and summed in bfloat16 or wider, within the bound.
A program may use at most 128 MiB of HBM per device.

```python
import math
import jax
import jax.numpy as jnp
from jax import lax

POL = 4
TAPS = 2048
SUBLEN = 16
BEAMS = 16
REACH = 8
RBLOCK = 128
FBEAMS = 128
CAP = 2
PULSES = 128
RANGE = 16384
SUBS = 2
MSUBS = 1
CHILD = 32
NBLK = 16
PBLOCKS = 4
FOOT = 128


def draw_footprint(key, part):
    tiles = FOOT // NBLK
    hottest = jax.random.randint(jax.random.fold_in(key, 7), (), 0, tiles)

    def one_device(device):
        dev_key = jax.random.fold_in(key, device + 11)
        first_key, second_key = jax.random.split(dev_key)
        others = jnp.arange((tiles - 1) * CAP, dtype=jnp.int32) // CAP
        others = others + (others >= hottest).astype(jnp.int32)
        others = jax.random.permutation(first_key, others)
        chosen = jnp.concatenate([jnp.zeros((CAP,), jnp.int32) + hottest, others[:NBLK - CAP]])
        return jax.random.permutation(second_key, chosen)
    listing = jax.vmap(one_device)(jnp.arange(PBLOCKS * tiles, dtype=jnp.int32))
    return listing.reshape(PBLOCKS, FOOT).astype(jnp.int32)


def touch_ends(result, rng, low, high):
    longest = result.shape.index(max(result.shape))
    spots = []
    for shift in (0, 1):
        where = [jax.random.randint(jax.random.fold_in(rng, axis), (), 0, length) for axis, length in enumerate(result.shape)]
        where[longest] = (where[longest] + shift) % result.shape[longest]
        spots.append(tuple(where))
    return result.at[spots[0]].set(low).at[spots[1]].set(high)


def level_of(own_key, dims, cuts, smallest, top_value):
    def one(axis_at, parts):
        draws = jax.random.uniform(jax.random.fold_in(jax.random.fold_in(own_key, 6), axis_at), (parts,), jnp.float32, smallest / len(cuts), top_value / len(cuts))
        return jnp.repeat(jnp.exp(draws), dims[axis_at] // parts).reshape((-1,) + (1,) * (len(dims) - axis_at - 1))

    loudness = one(*cuts[0])
    for cut in cuts[1:]:
        loudness = loudness * one(*cut)
    return loudness


def centred(own_key, shape, width, bound, cuts=(), kind=jnp.bfloat16):
    entries = width * jax.random.normal(own_key, shape, jnp.float32)
    if cuts:
        entries = entries * level_of(own_key, shape, cuts, -0.22, 0.18)
    return jnp.clip(entries, -bound, bound).astype(kind)


def setup_inputs(seed: int = 0) -> dict:
    key_list = jax.random.split(jax.random.key(seed), 11)
    echoes = centred(key_list[0], (2, PULSES, POL, RANGE), 1.0, 6.0, ((1, 4), (3, 8)))
    replica = centred(key_list[1], (2, TAPS), (2 * TAPS) ** -0.5, 0.09375)
    steer_phase = jnp.clip(jax.random.uniform(key_list[2], (BEAMS, SUBLEN), jnp.float32, -3.140625, 3.140625), -3.140625, 3.140625)
    range_shift = touch_ends(jax.random.randint(key_list[3], (2, 2 * BEAMS), 0 - REACH, REACH), jax.random.fold_in(key_list[3], 1), 0 - REACH, REACH - 1).astype(jnp.int32)
    merge_phase = jnp.clip(jax.random.uniform(key_list[4], (2, 2 * BEAMS), jnp.float32, -3.140625, 3.140625), -3.140625, 3.140625)
    merge_frac = jnp.clip(jax.random.uniform(key_list[5], (2, 2 * BEAMS), jnp.float32, 0.0, 1.0), 0.0, 1.0)
    footprint = draw_footprint(jax.random.fold_in(key_list[10], 71), 0)
    row_slot = touch_ends(jax.random.randint(key_list[7], (PBLOCKS, FOOT), 0, NBLK), jax.random.fold_in(key_list[7], 1), 0, NBLK - 1).astype(jnp.int32)
    beam_index = touch_ends(jax.random.randint(key_list[8], (PBLOCKS, FOOT, FBEAMS), 0, CHILD - 1), jax.random.fold_in(key_list[8], 1), 0, (CHILD - 1) - 1).astype(jnp.int32)
    beam_frac = jnp.clip(1.0 * jax.random.uniform(key_list[9], (PBLOCKS, FOOT, FBEAMS), jnp.float32) ** level_of(key_list[9], (PBLOCKS, FOOT, FBEAMS), ((0, 4), (1, 8)), -0.2, 0.2), 0.0, 1.0).astype(jnp.bfloat16)
    return dict(echoes=echoes, replica=replica, steer_phase=steer_phase, range_shift=range_shift, merge_phase=merge_phase, merge_frac=merge_frac, footprint=footprint, row_slot=row_slot, beam_index=beam_index, beam_frac=beam_frac)


def merge_pairs(padded, range_shift, merge_phase, merge_frac, extent):
    half_root = math.sqrt(0.5)
    total = None
    for parity in range(2):
        source = padded[:, parity::2]

        def single(beam_at, shift_at, angle, weight):
            picked = lax.dynamic_index_in_dim(source, beam_at // 2, axis=3, keepdims=False)
            lower_bins = lax.dynamic_slice_in_dim(picked, shift_at + REACH, extent, axis=3).astype(jnp.float32)
            upper_bins = lax.dynamic_slice_in_dim(picked, shift_at + REACH + 1, extent, axis=3).astype(jnp.float32)
            blended = (1.0 - weight) * lower_bins + weight * upper_bins
            cosine = jnp.cos(angle) * half_root
            sine = jnp.sin(angle) * half_root
            return jnp.stack([cosine * blended[0] - sine * blended[1], cosine * blended[1] + sine * blended[0]])
        beam_ids = jnp.arange(range_shift.shape[1], dtype=jnp.int32)
        branch = jax.vmap(single, out_axes=3)(beam_ids, range_shift[parity], merge_phase[parity], merge_frac[parity])
        total = branch if total is None else total + branch
    return total

def reference(echoes, replica, steer_phase, range_shift, merge_phase, merge_frac, footprint, row_slot, beam_index, beam_frac):
    tap_count = replica.shape[1]
    total_range = echoes.shape[3]
    fft_length = total_range + tap_count
    signal = echoes[0].astype(jnp.float32) + 1j * echoes[1].astype(jnp.float32)
    kernel = replica[0].astype(jnp.float32) + 1j * replica[1].astype(jnp.float32)
    spectrum = jnp.fft.fft(signal, n=fft_length, axis=-1) * jnp.conj(jnp.fft.fft(kernel, n=fft_length))
    correlated = jnp.fft.ifft(spectrum, axis=-1)[..., :total_range]
    compressed = jnp.stack([correlated.real, correlated.imag]).astype(jnp.bfloat16)
    scale = 1.0 / math.sqrt(SUBLEN)
    steer_re = (jnp.cos(steer_phase) * scale).astype(jnp.bfloat16).astype(jnp.float32)
    steer_im = (jnp.sin(steer_phase) * scale).astype(jnp.bfloat16).astype(jnp.float32)
    grouped_all = compressed.reshape(2, PBLOCKS, SUBS, SUBLEN, POL, total_range).transpose(1, 0, 2, 3, 4, 5)

    def per_block(accum, items):
        grouped, foot, rows_at, index_tab, frac_tab = items
        grouped = grouped.astype(jnp.float32)
        sub_re = jnp.einsum('ap,spqr->sqar', steer_re, grouped[0]) - jnp.einsum('ap,spqr->sqar', steer_im, grouped[1])
        sub_im = jnp.einsum('ap,spqr->sqar', steer_re, grouped[1]) + jnp.einsum('ap,spqr->sqar', steer_im, grouped[0])
        subimage = jnp.stack([sub_re, sub_im]).astype(jnp.bfloat16)
        padded = jnp.pad(subimage, ((0, 0), (0, 0), (0, 0), (0, 0), (REACH, REACH)))
        merged = merge_pairs(padded, range_shift, merge_phase, merge_frac, total_range).astype(jnp.bfloat16)
        children = merged.reshape(2, MSUBS, POL, 2 * BEAMS, FOOT, RBLOCK).transpose(4, 0, 2, 1, 3, 5)
        children = children.reshape(FOOT, 2, POL, CHILD, RBLOCK)
        lower = (1.0 - frac_tab.astype(jnp.float32)).astype(jnp.bfloat16)
        full_shape = (FOOT, 2, POL, FBEAMS, RBLOCK)
        low_index = jnp.broadcast_to(index_tab[:, None, None, :, None], full_shape)
        low_vals = jnp.take_along_axis(children, low_index, axis=3).astype(jnp.float32)
        high_vals = jnp.take_along_axis(children, low_index + 1, axis=3).astype(jnp.float32)
        resampled = lower.astype(jnp.float32)[:, None, None, :, None] * low_vals + frac_tab.astype(jnp.float32)[:, None, None, :, None] * high_vals
        segment = (foot * NBLK + rows_at).astype(jnp.int32)
        placed = jax.ops.segment_sum(resampled, segment, num_segments=FOOT)
        partial_value = placed.transpose(1, 2, 3, 0, 4).reshape(2, POL, FBEAMS, total_range).astype(jnp.bfloat16)
        return (accum + partial_value.astype(jnp.float32), None)
    start_image = jnp.zeros((2, POL, FBEAMS, total_range), jnp.float32)
    summed, _ = lax.scan(per_block, start_image, (grouped_all, footprint, row_slot, beam_index, beam_frac))
    return summed.astype(jnp.bfloat16)
```

```python
import functools
import math

import jax
import jax.numpy as jnp
from jax import lax
from jax.experimental import pallas as pl
from jax.experimental.pallas import tpu as pltpu
from jax.sharding import PartitionSpec as P

RBLOCK = 128
CAP = 2
CBLOCK = 256
EDGE = 128
TABROWS = 16


def shifted(value, axis, by):
    count = lax.axis_size(axis)
    pairs = [(i, i + by) for i in range(count) if 0 <= i + by < count]
    return lax.ppermute(value, axis, pairs)


def iota(shape, dim):
    return lax.broadcasted_iota(jnp.int32, shape, dim)


def form_kernel(
    shift_ref, coef_ref, foot_ref, slot_ref,
    own_ref, next_ref, prev_ref, after_ref, replica_ref, steer_ref, index_ref, frac_ref,
    kid_ref, tab_ref,
    ext_ref, toep_ref, sub_ref, merged_ref,
):
    range_dev = own_ref.shape[2]
    rows = own_ref.shape[1]
    taps = replica_ref.shape[1]
    window = CBLOCK + taps
    width = sub_ref.shape[1]
    blocks = range_dev // RBLOCK
    bf16 = jnp.bfloat16

    ext_ref[:, :, 0:EDGE] = prev_ref[...]
    ext_ref[:, :, EDGE : EDGE + range_dev] = own_ref[...]
    ext_ref[:, :, EDGE + range_dev : EDGE + 2 * range_dev] = next_ref[...]
    ext_ref[:, :, EDGE + 2 * range_dev :] = after_ref[...]

    for part in range(2):
        line = replica_ref[part : part + 1, :].astype(jnp.float32)
        line = jnp.concatenate([line, jnp.zeros((1, CBLOCK), jnp.float32)], axis=1)
        rolled = pltpu.roll(
            jnp.broadcast_to(line, (CBLOCK, window)), 0, 1, stride=1, stride_axis=0
        )
        if part == 0:
            toep_ref[0:CBLOCK, 0:window] = rolled.astype(bf16)
            toep_ref[CBLOCK:, window:] = rolled.astype(bf16)
        else:
            toep_ref[0:CBLOCK, window:] = rolled.astype(bf16)
            toep_ref[CBLOCK:, 0:window] = (-rolled).astype(bf16)

    r_at = iota((256, 32), 0)
    left = (((r_at >> 2) & 1) * 16 + ((r_at >> 3) & 15) == iota((256, 32), 1)).astype(bf16)
    k_at = iota((32, 256), 1)
    right = ((k_at >> 7) * 16 + ((k_at >> 2) & 15) == iota((32, 256), 0)).astype(bf16)
    spread = jnp.dot(left, steer_ref[...], preferred_element_type=jnp.float32).astype(bf16)
    spread = jnp.dot(spread, right, preferred_element_type=jnp.float32)
    r_all, k_all = iota((256, 256), 0), iota((256, 256), 1)
    same = ((r_all >> 7) == ((k_all >> 6) & 1)) & ((r_all & 3) == (k_all & 3))
    steer = jnp.where(same, spread, 0.0).astype(bf16)

    group = 3

    def compress(at, carry):
        pieces = []
        for step in range(group):
            start = pl.multiple_of((at * group + step) * CBLOCK, CBLOCK)
            pieces.append(
                jnp.concatenate(
                    [ext_ref[0, :, pl.ds(start, window)], ext_ref[1, :, pl.ds(start, window)]],
                    axis=1,
                )
            )
        left_side = jnp.concatenate(pieces, axis=0)
        found = lax.dot_general(
            left_side, toep_ref[...], (((1,), (1,)), ((), ())),
            preferred_element_type=jnp.float32,
        ).astype(bf16)
        for step in range(group):
            start = pl.multiple_of((at * group + step) * CBLOCK, CBLOCK)
            one = found[step * rows : (step + 1) * rows]
            stacked = jnp.concatenate([one[:, :CBLOCK], one[:, CBLOCK:]], axis=0)
            sub = jnp.dot(steer, stacked, preferred_element_type=jnp.float32)
            sub_ref[:, pl.ds(start, CBLOCK)] = sub.astype(bf16).astype(jnp.float32)
        return carry

    lax.fori_loop(0, width // (CBLOCK * group), compress, 0)

    @pl.when(lax.axis_index("tile") == 0)
    def _():
        sub_ref[:, 0:EDGE] = jnp.zeros((256, EDGE), jnp.float32)

    sign = jnp.where(iota((8, width), 0) < 4, -1.0, 1.0).astype(jnp.float32)

    def merge(a, carry):
        totals = [None, None]
        for c in range(2):
            x = sub_ref[pl.ds(pl.multiple_of((c * 16 + a) * 8, 8), 8), :]
            x_up = pltpu.roll(x, width - 1, 1)
            for parity in range(2):
                b = 2 * a + parity
                weight = coef_ref[0, c * 32 + b]
                cosine = coef_ref[1, c * 32 + b]
                sine = coef_ref[2, c * 32 + b]
                y = (1.0 - weight) * x + weight * x_up
                v = cosine * y + (sine * sign) * pltpu.roll(y, 4, 0)
                by = shift_ref[c, b]
                z = pltpu.roll(v, jnp.where(by > 0, width - by, -by), 1)
                z = z[:, EDGE : EDGE + range_dev]
                totals[parity] = z if totals[parity] is None else totals[parity] + z
        merged_ref[pl.ds(pl.multiple_of(a * 16, 16), 16), :] = jnp.concatenate(
            totals, axis=0
        ).astype(bf16)
        return carry

    lax.fori_loop(0, 16, merge, 0)

    order = (k_all == (r_all & 31) * 8 + (r_all >> 5)).astype(bf16)
    if tab_ref.shape[0] > blocks:
        kid_ref[...] = jnp.zeros(kid_ref.shape, bf16)
        tab_ref[...] = jnp.zeros(tab_ref.shape, bf16)
    tab_row = iota((TABROWS, RBLOCK), 0)
    for f in range(blocks):
        foot = foot_ref[0, f]
        rank = jnp.int32(0)
        for before in range(f):
            rank = rank + (foot_ref[0, before] == foot).astype(jnp.int32)
        slot = foot * CAP + rank
        part = jnp.dot(
            order, merged_ref[:, f * RBLOCK : (f + 1) * RBLOCK],
            preferred_element_type=jnp.float32,
        )
        kid_ref[:, slot] = part.astype(bf16).reshape(8, 32, RBLOCK)
        landing = (slot_ref[0, f] + 1).astype(jnp.float32)
        index_f = index_ref[0, f : f + 1, :].astype(jnp.float32)
        frac_f = frac_ref[0, f : f + 1, :].astype(jnp.float32)
        table = jnp.where(tab_row == 0, index_f, jnp.where(tab_row == 1, frac_f, 0.0))
        table = jnp.where(tab_row == 2, landing, table)
        tab_ref[slot] = table.astype(bf16)


def place_kernel(got_ref, out_ref, left_ref, right_ref):
    slots = got_ref.shape[0]
    beams = out_ref.shape[1]
    spans = out_ref.shape[2] // RBLOCK
    lanes = spans * beams
    mine = lax.axis_index("pulse") * beams
    bf16 = jnp.bfloat16
    lane = iota((RBLOCK, lanes), 1)
    widen = ((lane & (beams - 1)) + mine == iota((RBLOCK, lanes), 0)).astype(bf16)
    where_at = iota((1, lanes), 1) // beams + 1
    child = iota((32, lanes), 0).astype(jnp.float32)

    def prepare(at, carry):
        table = got_ref[at, 256 : 256 + TABROWS, :]
        wide = jnp.dot(table, widen, preferred_element_type=jnp.float32)
        landing = wide[2:3, :]
        index = jnp.where(landing == where_at.astype(jnp.float32), wide[0:1, :], -9.0)
        frac = wide[1:2, :]
        lower = (1.0 - frac).astype(bf16).astype(jnp.float32)
        weight = jnp.where(child == index, lower, 0.0)
        weight = jnp.where(child == index + 1.0, frac, weight)
        start = pl.multiple_of(at * 32, 32)
        left_ref[pl.ds(start, 32), :] = weight.astype(bf16)
        for x in range(8):
            right_ref[pl.ds(start, 32), x * RBLOCK : (x + 1) * RBLOCK] = got_ref[
                at, x * 32 : (x + 1) * 32, :
            ]
        return carry

    lax.fori_loop(0, slots, prepare, 0)
    for half in range(0, lanes, 256):
        result = lax.dot_general(
            left_ref[:, half : half + 256], right_ref[...], (((0,), (0,)), ((), ())),
            preferred_element_type=jnp.float32,
        ).astype(bf16)
        for sub in range(256 // beams):
            w = half // beams + sub
            for x in range(8):
                out_ref[x, :, w * RBLOCK : (w + 1) * RBLOCK] = result[
                    sub * beams : (sub + 1) * beams, x * RBLOCK : (x + 1) * RBLOCK
                ]


MESH = pl.DeviceIdType.MESH
POLS = 4
RAW = 2
UNITS = POLS + RAW
TAB = POLS
QUARTERS = 4
UNROLL = 4


def fused_kernel(
    tiles, shift_ref, blend_ref, foot_ref, slot_ref,
    echo_ref, replica_ref, steer_ref, phase_ref, index_ref, frac_ref, out_ref,
    ext_ref, toep_ref, big_ref, perm_ref, sub_ref, merged_ref, block_ref, kid_ref, tab_ref, wide_ref,
    kids, tabs, packed_ref, left_ref, part_ref, arrived_ref, own_ref,
    far_foot,
    local_sem, foot_sem, raw_send, raw_recv, halo_send, halo_recv,
    a2a_send, a2a_recv, line_send, line_recv, part_send, part_recv,
):
    g = lax.axis_index("pulse")
    t = lax.axis_index("tile")
    beams = out_ref.shape[2]
    range_dev = out_ref.shape[3]
    spans = range_dev // RBLOCK
    lanes = spans * beams
    slots = tiles * CAP
    depth = slots * 32
    pulses = echo_ref.shape[2]
    taps = replica_ref.shape[1]
    window = CBLOCK + taps
    blocks = spans

    bf16 = jnp.bfloat16
    f32 = jnp.float32
    is_mid = (g == 1) | (g == 2)
    inner = jnp.where(g == 0, 1, jnp.where(g == 1, 2, jnp.where(g == 2, 1, 2)))
    end = jnp.where(g < 2, 0, 3)
    far = 3 - end

    barrier = pltpu.get_barrier_semaphore()
    for d in range(1, tiles):
        pl.semaphore_signal(
            barrier, inc=1, device_id={"tile": lax.rem(t + d, tiles)}, device_id_type=MESH
        )
    pl.semaphore_signal(barrier, inc=1, device_id={"pulse": inner}, device_id_type=MESH)

    @pl.when(is_mid)
    def _():
        pl.semaphore_signal(barrier, inc=1, device_id={"pulse": end}, device_id_type=MESH)

    def local_copy(u):
        return pltpu.make_async_copy(
            echo_ref.at[:, u], ext_ref.at[u, :, :, pl.ds(EDGE, range_dev)], local_sem.at[u]
        )

    for u in range(POLS):
        local_copy(u).start()

    @pl.when(is_mid)
    def _():
        pl.semaphore_wait(barrier, tiles + 1)

    @pl.when(jnp.logical_not(is_mid))
    def _():
        pl.semaphore_wait(barrier, tiles)

    halos = [
        ((0, range_dev), EDGE + range_dev, -1),
        ((range_dev - EDGE, EDGE), 0, 1),
        ((0, EDGE), EDGE + 2 * range_dev, -2),
    ]

    def halo_copy(u, j, forward=False):
        (first, count), to, by = halos[j]
        if forward:
            src = ext_ref.at[u, :, :, pl.ds(EDGE + first, count)]
        else:
            src = echo_ref.at[:, u, :, pl.ds(first, count)]
        return pltpu.make_async_remote_copy(
            src_ref=src,
            dst_ref=ext_ref.at[u, :, :, pl.ds(to, count)],
            send_sem=halo_send.at[u, j], recv_sem=halo_recv.at[u, j],
            device_id={"tile": lax.rem(t + by + tiles, tiles)}, device_id_type=MESH,
        )

    def sends(j):
        by = halos[j][2]
        return (t + by >= 0) & (t + by < tiles)

    def gets(j):
        by = halos[j][2]
        return (t - by >= 0) & (t - by < tiles)

    def halo_start(u, forward=False):
        for j in range(3):
            @pl.when(sends(j))
            def _():
                halo_copy(u, j, forward).start()

    def raw_copy(i):
        return pltpu.make_async_remote_copy(
            src_ref=echo_ref.at[:, POLS - RAW + i],
            dst_ref=ext_ref.at[POLS + i, :, :, pl.ds(EDGE, range_dev)],
            send_sem=raw_send.at[i], recv_sem=raw_recv.at[i],
            device_id={"pulse": inner}, device_id_type=MESH,
        )

    def foot_copy():
        return pltpu.make_async_remote_copy(
            src_ref=foot_ref, dst_ref=far_foot, send_sem=foot_sem.at[0], recv_sem=foot_sem.at[1],
            device_id={"pulse": inner}, device_id_type=MESH,
        )

    halo_start(0)

    @pl.when(is_mid)
    def _():
        foot_copy().start()
        for i in range(RAW):
            raw_copy(i).start()

    for u in range(UNITS):
        for j in range(3):
            (_, count), to, _ = halos[j]

            @pl.when(jnp.logical_not(gets(j)))
            def _():
                ext_ref[u, :, :, to : to + count] = jnp.zeros((2, pulses, count), bf16)

    def order_blocks(feet):
        targets = []
        for f in range(blocks):
            rank = jnp.int32(0)
            for earlier in range(f):
                rank = rank + (feet[earlier] == feet[f]).astype(jnp.int32)
            targets.append(feet[f] * CAP + rank)
        sources = []
        for s in range(slots):
            source = jnp.int32(0)
            for f in range(blocks):
                source = source + f * (targets[f] == s).astype(jnp.int32)
            sources.append(source)
        return sources

    @pl.when(jnp.logical_not(is_mid))
    def _():
        for f in range(blocks):
            far_foot[0, f] = jnp.int32(0)

    sources = order_blocks([foot_ref[0, f] for f in range(blocks)])
    tab_row = iota((TABROWS, RBLOCK), 0)
    for f in range(blocks):
        index_f = index_ref[0, f : f + 1, :].astype(f32)
        frac_f = frac_ref[0, f : f + 1, :].astype(f32)
        landing = (slot_ref[0, f] + 1).astype(f32)
        table = jnp.where(tab_row == 0, index_f, jnp.where(tab_row == 1, frac_f, 0.0))
        wide_ref[f] = jnp.where(tab_row == 2, landing, table).astype(bf16)
    for s in range(slots):
        tab_ref[s] = wide_ref[sources[s]]

    def tab_copy(d, peer, place):
        return pltpu.make_async_remote_copy(
            src_ref=tab_ref.at[pl.ds(peer * CAP, CAP)],
            dst_ref=tabs.at[pl.ds(place * CAP, CAP)],
            send_sem=a2a_send.at[UNITS, d - 1], recv_sem=a2a_recv.at[UNITS, d - 1],
            device_id={"tile": peer}, device_id_type=MESH,
        )

    def unit_place(u):
        return jnp.where(u < POLS, g, inner), jnp.where(u < POLS, u, u - RAW)

    def spread_copy(u, d, peer, place):
        group, pol = unit_place(u)
        return pltpu.make_async_remote_copy(
            src_ref=kid_ref.at[u, :, pl.ds(peer * CAP, CAP)],
            dst_ref=kids.at[group, pol, :, pl.ds(place * CAP, CAP)],
            send_sem=a2a_send.at[u, d - 1], recv_sem=a2a_recv.at[u, d - 1],
            device_id={"tile": peer}, device_id_type=MESH,
        )

    def spread_start(u):
        for d in range(1, tiles):
            spread_copy(u, d, lax.rem(t + d, tiles), t).start()
        group, pol = unit_place(u)
        kids[group, pol, :, pl.ds(t * CAP, CAP)] = kid_ref[u, :, pl.ds(t * CAP, CAP)]

    def spread_wait(u):
        for d in range(1, tiles):
            peer = lax.rem(t + tiles - d, tiles)
            spread_copy(u, d, peer, peer).wait_recv()

    def line_copy(k, group, lane, to):
        part = kids.at[group, k]
        return pltpu.make_async_remote_copy(
            src_ref=part, dst_ref=part,
            send_sem=line_send.at[lane, k], recv_sem=line_recv.at[group, k],
            device_id={"pulse": to}, device_id_type=MESH,
        )

    def line_tab(group, lane, to):
        part = packed_ref.at[group]
        return pltpu.make_async_remote_copy(
            src_ref=part, dst_ref=part,
            send_sem=line_send.at[lane, TAB], recv_sem=line_recv.at[group, TAB],
            device_id={"pulse": to}, device_id_type=MESH,
        )

    for d in range(1, tiles):
        tab_copy(d, lax.rem(t + d, tiles), t).start()
    tabs[pl.ds(t * CAP, CAP)] = tab_ref[pl.ds(t * CAP, CAP)]

    for part in range(2):
        line = replica_ref[part : part + 1, :].astype(f32)
        line = jnp.concatenate([line, jnp.zeros((1, CBLOCK), f32)], axis=1)
        rolled = pltpu.roll(
            jnp.broadcast_to(line, (CBLOCK, window)), 0, 1, stride=1, stride_axis=0
        )
        if part == 0:
            toep_ref[0:CBLOCK, 0:window] = rolled.astype(bf16)
            toep_ref[CBLOCK:, window:] = rolled.astype(bf16)
        else:
            toep_ref[0:CBLOCK, window:] = rolled.astype(bf16)
            toep_ref[CBLOCK:, 0:window] = (-rolled).astype(bf16)

    halo_start(1)

    row = iota((64, 16), 0)
    angle = jnp.zeros((64, 16), f32)
    for a in range(16):
        angle = jnp.where(((row >> 1) & 15) == a, steer_ref[a : a + 1, :], angle)
    on_row = iota((32, 32), 0) == iota((32, 32), 1)
    turns = [
        jnp.sum(jnp.where(on_row, phase_ref[c : c + 1, :], 0.0), axis=1, keepdims=True)
        for c in range(2)
    ]
    angle = angle + jnp.concatenate(turns, axis=0)
    scale = math.sqrt(0.5) / math.sqrt(steer_ref.shape[1])
    cosine, sine = jnp.cos(angle) * scale, jnp.sin(angle) * scale
    small = jnp.concatenate(
        [
            jnp.concatenate([cosine, -sine], axis=1),
            jnp.concatenate([sine, cosine], axis=1),
        ],
        axis=0,
    ).astype(bf16)
    o_at = iota((512, 128), 0)
    tall = ((o_at & 1) * 64 + (o_at >> 3) == iota((512, 128), 1)).astype(bf16)
    i_at = iota((32, 256), 1)
    broad = (((i_at >> 5) & 1) * 16 + (i_at & 15) == iota((32, 256), 0)).astype(bf16)
    spread = jnp.dot(tall, small, preferred_element_type=f32).astype(bf16)
    spread = jnp.dot(spread, broad, preferred_element_type=f32)
    o_all, i_all = iota((512, 256), 0), iota((512, 256), 1)
    same = (((o_all >> 1) & 3) == (i_all >> 6)) & ((o_all >> 8) == ((i_all >> 4) & 1))
    big_ref[...] = jnp.where(same, spread, 0.0).astype(bf16)
    o_all, i_all = iota((256, 256), 0), iota((256, 256), 1)
    order_in = (o_all & 31) * 8 + ((o_all >> 5) & 3) * 2 + (o_all >> 7)
    perm_ref[...] = (i_all == order_in).astype(bf16)

    @pl.when(is_mid)
    def _():
        foot_copy().wait_recv()

    far_sources = order_blocks([far_foot[0, f] for f in range(blocks)])

    def begin_tab():
        for d in range(1, tiles):
            peer = lax.rem(t + tiles - d, tiles)
            tab_copy(d, peer, peer).wait_recv()
        row, column = iota((3 * slots, slots * TABROWS), 0), iota((3 * slots, slots * TABROWS), 1)
        choose = column == (row & (slots - 1)) * TABROWS + row // slots
        packed_ref[g] = jnp.dot(
            choose.astype(bf16), tabs[...].reshape(slots * TABROWS, RBLOCK),
            preferred_element_type=f32,
        ).astype(bf16)
        line_tab(g, 0, inner).start()

    def relay(k):
        line_copy(k, end, 0, inner).wait_recv()
        line_copy(k, end, 1, inner).start()

    def form(u):
        @pl.when(u < POLS)
        def _():
            local_copy(u).wait()

        for j in range(3):
            @pl.when(gets(j))
            def _():
                halo_copy(u, j, True).wait_recv()

        pieces = []
        for j in range(9):
            start = j * CBLOCK
            pieces.append(
                jnp.concatenate(
                    [ext_ref[u, 0, :, start : start + window], ext_ref[u, 1, :, start : start + window]],
                    axis=1,
                )
            )
        found = lax.dot_general(
            jnp.concatenate(pieces, axis=0), toep_ref[...], (((1,), (1,)), ((), ())),
            preferred_element_type=f32,
        ).astype(bf16)
        before = (iota((pulses, 2 * CBLOCK), 1) & (CBLOCK - 1)) < EDGE
        first = jnp.where(before & (t == 0), 0.0, found[0:pulses].astype(f32)).astype(bf16)
        for jj in range(3):
            stacked = []
            for q in range(QUARTERS):
                at = 2 * q + jj
                one = first if at == 0 else found[at * pulses : (at + 1) * pulses]
                stacked += [one[:, :CBLOCK], one[:, CBLOCK:]]
            sub_ref[:, jj * CBLOCK : (jj + 1) * CBLOCK] = jnp.dot(
                big_ref[...], jnp.concatenate(stacked, axis=0), preferred_element_type=f32
            )

        def merge(b, carry):
            totals = [None] * 4
            for c in range(2):
                by = shift_ref[c, b]
                weight = blend_ref[c, b]
                back = by < 0
                turn = jnp.where(back, by + RBLOCK, by)
                x = sub_ref[pl.ds(pl.multiple_of((c * 32 + b) * 8, 8), 8), :]
                x = jnp.concatenate([x[:, i * RBLOCK : (i + 1) * RBLOCK] for i in range(6)], axis=0)
                x = jnp.where(back, x[:40], x[8:])
                low = pltpu.roll(x, (RBLOCK - turn) & (RBLOCK - 1), 1)
                high = pltpu.roll(x, RBLOCK - 1 - turn, 1)
                lane = iota((32, RBLOCK), 1)
                low = jnp.where(lane < RBLOCK - turn, low[:32], low[8:])
                high = jnp.where(lane < RBLOCK - 1 - turn, high[:32], high[8:])
                y = (1.0 - weight) * low + weight * high
                totals = y if c == 0 else totals + y
            for i in range(4):
                merged_ref[pl.ds(pl.multiple_of(b * 8, 8), 8), i * RBLOCK : (i + 1) * RBLOCK] = (
                    totals[i * 8 : (i + 1) * 8]
                )
            return carry

        lax.fori_loop(0, 32, merge, 0, unroll=UNROLL)
        ordered = jnp.dot(
            perm_ref[...], merged_ref[...].astype(bf16), preferred_element_type=f32
        ).astype(bf16)
        for part in range(2):
            for f in range(blocks):
                at = (part * QUARTERS + f // 4) * 32
                block_ref[f, part] = ordered[at : at + 32, (f % 4) * RBLOCK : (f % 4 + 1) * RBLOCK]
        for s in range(slots):
            kid_ref[u, :, s] = block_ref[jnp.where(u < POLS, sources[s], far_sources[s])]
        spread_start(u)

    def own_line(k):
        spread_wait(k)
        line_copy(k, g, 0, inner).start()

    def forward(i):
        raw_copy(i).wait_recv()
        halo_start(POLS + i, True)

    def mid_unit(u):
        return jnp.where(u == 3, 4, jnp.where(u == 4, 3, u))

    def step(i, carry):
        form(jnp.where(is_mid, mid_unit(i), i))

        @pl.when(i == 0)
        def _():
            begin_tab()

        @pl.when(jnp.logical_not(is_mid) & (i + 2 < POLS))
        def _():
            halo_start(i + 2)

        @pl.when(jnp.logical_not(is_mid) & (i >= 1))
        def _():
            own_line(i - 1)

        @pl.when(is_mid & (i == 1))
        def _():
            halo_start(2)
            own_line(0)
            forward(0)
            own_line(1)

        @pl.when(is_mid & (i == 2))
        def _():
            halo_start(3)
            line_tab(end, 0, inner).wait_recv()
            line_tab(end, 1, inner).start()
            forward(1)

        @pl.when(is_mid & (i >= 3))
        def _():
            relay(i - 3)

        return carry

    units = jnp.where(is_mid, UNITS, POLS)
    lax.fori_loop(0, units, step, 0)

    middle = spans // 2 * RBLOCK

    def part_copy(k, half, to):
        return pltpu.make_async_remote_copy(
            src_ref=part_ref.at[k, :, :, pl.ds(half * middle, middle)],
            dst_ref=arrived_ref.at[k, :, :, pl.ds(half * middle, middle)],
            send_sem=part_send.at[k, half], recv_sem=part_recv.at[k, half],
            device_id={"pulse": to}, device_id_type=MESH,
        )

    def prepare(group, beam_group, row, column, used):
        expand = (
            (iota((RBLOCK, lanes), 1) & (beams - 1)) + beam_group * beams
            == iota((RBLOCK, lanes), 0)
        ).astype(bf16)
        where_at = (iota((1, lanes), 1) // beams + 1).astype(f32)
        child = iota((32, lanes), 0).astype(f32)

        wide = jnp.dot(packed_ref[group], expand, preferred_element_type=f32)
        for at in range(slots // 4):
            pieces = []
            for slot in range(at * 4, at * 4 + 4):
                landing = wide[2 * slots + slot : 2 * slots + slot + 1, :]
                index = jnp.where(
                    (landing == where_at) & used, wide[slot : slot + 1, :], -9.0
                )
                frac = wide[slots + slot : slots + slot + 1, :]
                lower = (1.0 - frac).astype(bf16).astype(f32)
                weight = jnp.where(child == index, lower, 0.0)
                pieces.append(jnp.where(child == index + 1.0, frac, weight))
            block = jnp.concatenate(pieces, axis=0)
            at_column = pl.multiple_of(column + at * 128, 128)
            left_ref[row : row + lanes, pl.ds(at_column, 128)] = block.T.astype(bf16)

    @pl.when(is_mid)
    def _():
        line_tab(inner, 0, inner).wait_recv()
        line_tab(far, 0, inner).wait_recv()

        def prepare_group(group, carry):
            column = pl.multiple_of(group * depth, 128)
            prepare(group, g, 0, column, group >= 0)
            prepare(group, end, lanes, column, group != end)
            return carry

        lax.fori_loop(0, 4, prepare_group, 0)
        for u in range(POLS - RAW, UNITS):
            spread_wait(u)
        for k in range(POLS - RAW):
            line_copy(k, inner, 0, inner).wait_recv()

        def final(k, carry):
            @pl.when(k == 1)
            def _():
                relay(3)

            line_copy(k, far, 0, inner).wait_recv()
            right = jnp.concatenate(
                [kids[:, k, i].reshape(4 * depth, RBLOCK) for i in range(2)], axis=1
            )
            for half in range(2):
                first = lanes + half * (lanes // 2)
                result = jnp.dot(
                    left_ref[first : first + lanes // 2, :], right, preferred_element_type=f32
                ).astype(bf16)
                for step in range(spans // 2):
                    w = half * (spans // 2) + step
                    for i in range(2):
                        part_ref[k, i, :, w * RBLOCK : (w + 1) * RBLOCK] = result[
                            step * beams : (step + 1) * beams, i * RBLOCK : (i + 1) * RBLOCK
                        ]
                part_copy(k, half, end).start()
            result = jnp.dot(
                left_ref[:lanes, :], right, preferred_element_type=f32
            ).astype(bf16)
            for w in range(spans):
                for i in range(2):
                    out_ref[i, k, :, w * RBLOCK : (w + 1) * RBLOCK] = result[
                        w * beams : (w + 1) * beams, i * RBLOCK : (i + 1) * RBLOCK
                    ]
            return carry

        lax.fori_loop(0, POLS, final, 0)
        line_tab(g, 0, inner).wait_send()
        line_tab(end, 1, inner).wait_send()
        for k in range(POLS):
            if k < POLS - RAW:
                line_copy(k, g, 0, inner).wait_send()
            line_copy(k, end, 1, inner).wait_send()
            for half in range(2):
                part_copy(k, half, end).wait_send()
        foot_copy().wait_send()
        for i in range(RAW):
            raw_copy(i).wait_send()

    @pl.when(jnp.logical_not(is_mid))
    def _():
        spread_wait(POLS - 1)
        line_copy(POLS - 1, g, 0, inner).start()
        prepare(g, g, 0, 0, g >= 0)

        def product(k, carry):
            right = jnp.concatenate(
                [kids[g, k, i].reshape(depth, RBLOCK) for i in range(2)], axis=1
            )
            result = jnp.dot(left_ref[:lanes, :depth], right, preferred_element_type=f32)
            for w in range(spans):
                for i in range(2):
                    own_ref[k, i, :, w * RBLOCK : (w + 1) * RBLOCK] = result[
                        w * beams : (w + 1) * beams, i * RBLOCK : (i + 1) * RBLOCK
                    ]
            return carry

        lax.fori_loop(0, POLS, product, 0)

        def finish(k, carry):
            for half in range(2):
                part_copy(k, half, inner).wait_recv()
                span = slice(half * middle, (half + 1) * middle)
                for i in range(2):
                    out_ref[i, k, :, span] = (
                        own_ref[k, i, :, span] + arrived_ref[k, i, :, span].astype(f32)
                    ).astype(bf16)
            return carry

        lax.fori_loop(0, POLS, finish, 0)
        line_tab(g, 0, inner).wait_send()
        for k in range(POLS):
            line_copy(k, g, 0, inner).wait_send()

    for d in range(1, tiles):
        tab_copy(d, lax.rem(t + d, tiles), t).wait_send()

    def drain(u, carry):
        for d in range(1, tiles):
            spread_copy(u, d, lax.rem(t + d, tiles), t).wait_send()
        for j in range(3):
            @pl.when(sends(j))
            def _():
                halo_copy(u, j, True).wait_send()
        return carry

    lax.fori_loop(0, units, drain, 0)


def fused(
    shift, blend, foot, slot, echoes, replica, steer_phase, merge_phase, index, frac,
    tiles, beams, range_dev,
):
    slots = tiles * CAP
    lanes = range_dev // RBLOCK * beams
    bf16 = jnp.bfloat16
    f32 = jnp.float32
    pulses = echoes.shape[2]
    vmem = pl.BlockSpec(memory_space=pltpu.VMEM)
    smem = pl.BlockSpec(memory_space=pltpu.SMEM)
    dma = pltpu.SemaphoreType.DMA
    return pl.pallas_call(
        functools.partial(fused_kernel, tiles),
        out_shape=jax.ShapeDtypeStruct((2, POLS, beams, range_dev), bf16),
        in_specs=[smem] * 4 + [pl.BlockSpec(memory_space=pl.ANY)] + [vmem] * 5,
        out_specs=vmem,
        scratch_shapes=[
            pltpu.VMEM((UNITS, 2, pulses, 2 * range_dev + 2 * EDGE), bf16),
            pltpu.VMEM((2 * CBLOCK, 2 * (CBLOCK + replica.shape[1])), bf16),
            pltpu.VMEM((512, 256), bf16),
            pltpu.VMEM((256, 256), bf16),
            pltpu.VMEM((512, 3 * CBLOCK), f32),
            pltpu.VMEM((256, 4 * RBLOCK), f32),
            pltpu.VMEM((slots, 2, 32, RBLOCK), bf16),
            pltpu.VMEM((UNITS, 2, slots, 32, RBLOCK), bf16),
            pltpu.VMEM((slots, TABROWS, RBLOCK), bf16),
            pltpu.VMEM((slots, TABROWS, RBLOCK), bf16),
            pltpu.VMEM((4, POLS, 2, slots, 32, RBLOCK), bf16),
            pltpu.VMEM((slots, TABROWS, RBLOCK), bf16),
            pltpu.VMEM((4, 3 * slots, RBLOCK), bf16),
            pltpu.VMEM((2 * lanes, 4 * slots * 32), bf16),
            pltpu.VMEM((POLS, 2, beams, range_dev), bf16),
            pltpu.VMEM((POLS, 2, beams, range_dev), bf16),
            pltpu.VMEM((POLS, 2, beams, range_dev), f32),
            pltpu.SMEM((1, range_dev // RBLOCK), jnp.int32),
            dma((POLS,)),
            dma((2,)),
            dma((RAW,)),
            dma((RAW,)),
            dma((UNITS, 3)),
            dma((UNITS, 3)),
            dma((UNITS + 1, tiles - 1)),
            dma((UNITS + 1, tiles - 1)),
            dma((2, POLS + 1)),
            dma((4, POLS + 1)),
            dma((POLS, 2)),
            dma((POLS, 2)),
        ],
        compiler_params=pltpu.CompilerParams(
            collective_id=0, has_side_effects=True, vmem_limit_bytes=40 << 20
        ),
    )(shift, blend, foot, slot, echoes, replica, steer_phase, merge_phase, index, frac)


def shards(
    echoes, replica, steer_phase, range_shift, merge_phase, merge_frac,
    footprint, row_slot, beam_index, beam_frac,
):
    pulse_count, pol_count, range_dev = echoes.shape[1:]
    rows = pulse_count * pol_count
    taps = replica.shape[1]
    final_beams = beam_index.shape[2]
    tiles = lax.axis_size("tile")
    groups = lax.axis_size("pulse")
    slot_count = tiles * CAP
    scale = 1.0 / math.sqrt(steer_phase.shape[1])
    steer_re = jnp.cos(steer_phase) * scale
    steer_im = jnp.sin(steer_phase) * scale
    steer = jnp.concatenate(
        [
            jnp.concatenate([steer_re, -steer_im], axis=1),
            jnp.concatenate([steer_im, steer_re], axis=1),
        ],
        axis=0,
    ).astype(jnp.bfloat16)
    half_root = math.sqrt(0.5)
    coef = jnp.stack(
        [
            merge_frac.reshape(-1),
            (jnp.cos(merge_phase) * half_root).reshape(-1),
            (jnp.sin(merge_phase) * half_root).reshape(-1),
        ]
    )
    beams = final_beams // groups
    if groups == 4 and slot_count == range_dev // RBLOCK:
        return fused(
            range_shift, merge_frac, footprint, row_slot, echoes.transpose(0, 2, 1, 3),
            replica, steer_phase, merge_phase, beam_index, beam_frac, tiles, beams, range_dev,
        )
    own = echoes.reshape(2, rows, range_dev)
    following = shifted(own, "tile", -1)
    before = shifted(own[:, :, range_dev - EDGE :], "tile", 1)
    after = shifted(own[:, :, :EDGE], "tile", -2)

    width = range_dev + CBLOCK
    smem = pl.BlockSpec(memory_space=pltpu.SMEM)
    vmem = pl.BlockSpec(memory_space=pltpu.VMEM)
    kids, tabs = pl.pallas_call(
        form_kernel,
        out_shape=(
            jax.ShapeDtypeStruct((8, slot_count, 32, RBLOCK), jnp.bfloat16),
            jax.ShapeDtypeStruct((slot_count, TABROWS, RBLOCK), jnp.bfloat16),
        ),
        in_specs=[smem] * 4 + [vmem] * 8,
        out_specs=(vmem, vmem),
        scratch_shapes=[
            pltpu.VMEM((2, rows, 2 * range_dev + 2 * EDGE), jnp.bfloat16),
            pltpu.VMEM((2 * CBLOCK, 2 * (CBLOCK + taps)), jnp.bfloat16),
            pltpu.VMEM((256, width), jnp.float32),
            pltpu.VMEM((256, range_dev), jnp.bfloat16),
        ],
        compiler_params=pltpu.CompilerParams(vmem_limit_bytes=56 << 20),
    )(
        range_shift, coef, footprint, row_slot,
        own, following, before, after, replica, steer, beam_index, beam_frac,
    )
    sent = jnp.concatenate(
        [kids.transpose(1, 0, 2, 3).reshape(slot_count, 256, RBLOCK), tabs], axis=1
    )
    got = lax.all_to_all(
        sent.reshape(tiles, CAP, 256 + TABROWS, RBLOCK), "tile",
        split_axis=0, concat_axis=0, tiled=True,
    ).reshape(slot_count, 256 + TABROWS, RBLOCK)
    gathered = lax.all_gather(got, "pulse", axis=0, tiled=True)
    total_slots = groups * slot_count
    image = pl.pallas_call(
        place_kernel,
        out_shape=jax.ShapeDtypeStruct((2 * pol_count, beams, range_dev), jnp.bfloat16),
        in_specs=[vmem],
        out_specs=vmem,
        scratch_shapes=[
            pltpu.VMEM((total_slots * 32, range_dev // RBLOCK * beams), jnp.bfloat16),
            pltpu.VMEM((total_slots * 32, 8 * RBLOCK), jnp.bfloat16),
        ],
        compiler_params=pltpu.CompilerParams(vmem_limit_bytes=56 << 20),
    )(gathered)
    return image.reshape(2, pol_count, beams, range_dev)


def solution(mesh):
    placed = (
        P(None, "pulse", None, "tile"),
        P(),
        P(),
        P(),
        P(),
        P(),
        P("pulse", "tile"),
        P("pulse", "tile"),
        P("pulse", "tile", None),
        P("pulse", "tile", None),
    )
    return jax.shard_map(
        shards,
        mesh=mesh,
        in_specs=placed,
        out_specs=P(None, None, "pulse", "tile"),
        check_vma=False,
    )
```

```python
import functools
import math

import jax
import jax.numpy as jnp
from jax import lax
from jax.experimental import pallas as pl
from jax.experimental.pallas import tpu as pltpu
from jax.sharding import PartitionSpec as P

RBLOCK = 128
CAP = 2
CBLOCK = 256
EDGE = 128
TABROWS = 16


def shifted(value, axis, by):
    count = lax.axis_size(axis)
    pairs = [(i, i + by) for i in range(count) if 0 <= i + by < count]
    return lax.ppermute(value, axis, pairs)


def iota(shape, dim):
    return lax.broadcasted_iota(jnp.int32, shape, dim)


def form_kernel(
    shift_ref, coef_ref, foot_ref, slot_ref,
    own_ref, next_ref, prev_ref, after_ref, replica_ref, steer_ref, index_ref, frac_ref,
    kid_ref, tab_ref,
    ext_ref, toep_ref, sub_ref, merged_ref,
):
    range_dev = own_ref.shape[2]
    rows = own_ref.shape[1]
    taps = replica_ref.shape[1]
    window = CBLOCK + taps
    width = sub_ref.shape[1]
    blocks = range_dev // RBLOCK
    bf16 = jnp.bfloat16

    ext_ref[:, :, 0:EDGE] = prev_ref[...]
    ext_ref[:, :, EDGE : EDGE + range_dev] = own_ref[...]
    ext_ref[:, :, EDGE + range_dev : EDGE + 2 * range_dev] = next_ref[...]
    ext_ref[:, :, EDGE + 2 * range_dev :] = after_ref[...]

    for part in range(2):
        line = replica_ref[part : part + 1, :].astype(jnp.float32)
        line = jnp.concatenate([line, jnp.zeros((1, CBLOCK), jnp.float32)], axis=1)
        rolled = pltpu.roll(
            jnp.broadcast_to(line, (CBLOCK, window)), 0, 1, stride=1, stride_axis=0
        )
        if part == 0:
            toep_ref[0:CBLOCK, 0:window] = rolled.astype(bf16)
            toep_ref[CBLOCK:, window:] = rolled.astype(bf16)
        else:
            toep_ref[0:CBLOCK, window:] = rolled.astype(bf16)
            toep_ref[CBLOCK:, 0:window] = (-rolled).astype(bf16)

    r_at = iota((256, 32), 0)
    left = (((r_at >> 2) & 1) * 16 + ((r_at >> 3) & 15) == iota((256, 32), 1)).astype(bf16)
    k_at = iota((32, 256), 1)
    right = ((k_at >> 7) * 16 + ((k_at >> 2) & 15) == iota((32, 256), 0)).astype(bf16)
    spread = jnp.dot(left, steer_ref[...], preferred_element_type=jnp.float32).astype(bf16)
    spread = jnp.dot(spread, right, preferred_element_type=jnp.float32)
    r_all, k_all = iota((256, 256), 0), iota((256, 256), 1)
    same = ((r_all >> 7) == ((k_all >> 6) & 1)) & ((r_all & 3) == (k_all & 3))
    steer = jnp.where(same, spread, 0.0).astype(bf16)

    group = 3

    def compress(at, carry):
        pieces = []
        for step in range(group):
            start = pl.multiple_of((at * group + step) * CBLOCK, CBLOCK)
            pieces.append(
                jnp.concatenate(
                    [ext_ref[0, :, pl.ds(start, window)], ext_ref[1, :, pl.ds(start, window)]],
                    axis=1,
                )
            )
        left_side = jnp.concatenate(pieces, axis=0)
        found = lax.dot_general(
            left_side, toep_ref[...], (((1,), (1,)), ((), ())),
            preferred_element_type=jnp.float32,
        ).astype(bf16)
        for step in range(group):
            start = pl.multiple_of((at * group + step) * CBLOCK, CBLOCK)
            one = found[step * rows : (step + 1) * rows]
            stacked = jnp.concatenate([one[:, :CBLOCK], one[:, CBLOCK:]], axis=0)
            sub = jnp.dot(steer, stacked, preferred_element_type=jnp.float32)
            sub_ref[:, pl.ds(start, CBLOCK)] = sub.astype(bf16).astype(jnp.float32)
        return carry

    lax.fori_loop(0, width // (CBLOCK * group), compress, 0)

    @pl.when(lax.axis_index("tile") == 0)
    def _():
        sub_ref[:, 0:EDGE] = jnp.zeros((256, EDGE), jnp.float32)

    sign = jnp.where(iota((8, width), 0) < 4, -1.0, 1.0).astype(jnp.float32)

    def merge(a, carry):
        totals = [None, None]
        for c in range(2):
            x = sub_ref[pl.ds(pl.multiple_of((c * 16 + a) * 8, 8), 8), :]
            x_up = pltpu.roll(x, width - 1, 1)
            for parity in range(2):
                b = 2 * a + parity
                weight = coef_ref[0, c * 32 + b]
                cosine = coef_ref[1, c * 32 + b]
                sine = coef_ref[2, c * 32 + b]
                y = (1.0 - weight) * x + weight * x_up
                v = cosine * y + (sine * sign) * pltpu.roll(y, 4, 0)
                by = shift_ref[c, b]
                z = pltpu.roll(v, jnp.where(by > 0, width - by, -by), 1)
                z = z[:, EDGE : EDGE + range_dev]
                totals[parity] = z if totals[parity] is None else totals[parity] + z
        merged_ref[pl.ds(pl.multiple_of(a * 16, 16), 16), :] = jnp.concatenate(
            totals, axis=0
        ).astype(bf16)
        return carry

    lax.fori_loop(0, 16, merge, 0)

    order = (k_all == (r_all & 31) * 8 + (r_all >> 5)).astype(bf16)
    if tab_ref.shape[0] > blocks:
        kid_ref[...] = jnp.zeros(kid_ref.shape, bf16)
        tab_ref[...] = jnp.zeros(tab_ref.shape, bf16)
    tab_row = iota((TABROWS, RBLOCK), 0)
    for f in range(blocks):
        foot = foot_ref[0, f]
        rank = jnp.int32(0)
        for before in range(f):
            rank = rank + (foot_ref[0, before] == foot).astype(jnp.int32)
        slot = foot * CAP + rank
        part = jnp.dot(
            order, merged_ref[:, f * RBLOCK : (f + 1) * RBLOCK],
            preferred_element_type=jnp.float32,
        )
        kid_ref[:, slot] = part.astype(bf16).reshape(8, 32, RBLOCK)
        landing = (slot_ref[0, f] + 1).astype(jnp.float32)
        index_f = index_ref[0, f : f + 1, :].astype(jnp.float32)
        frac_f = frac_ref[0, f : f + 1, :].astype(jnp.float32)
        table = jnp.where(tab_row == 0, index_f, jnp.where(tab_row == 1, frac_f, 0.0))
        table = jnp.where(tab_row == 2, landing, table)
        tab_ref[slot] = table.astype(bf16)


def place_kernel(got_ref, out_ref, left_ref, right_ref):
    slots = got_ref.shape[0]
    beams = out_ref.shape[1]
    spans = out_ref.shape[2] // RBLOCK
    lanes = spans * beams
    mine = lax.axis_index("pulse") * beams
    bf16 = jnp.bfloat16
    lane = iota((RBLOCK, lanes), 1)
    widen = ((lane & (beams - 1)) + mine == iota((RBLOCK, lanes), 0)).astype(bf16)
    where_at = iota((1, lanes), 1) // beams + 1
    child = iota((32, lanes), 0).astype(jnp.float32)

    def prepare(at, carry):
        table = got_ref[at, 256 : 256 + TABROWS, :]
        wide = jnp.dot(table, widen, preferred_element_type=jnp.float32)
        landing = wide[2:3, :]
        index = jnp.where(landing == where_at.astype(jnp.float32), wide[0:1, :], -9.0)
        frac = wide[1:2, :]
        lower = (1.0 - frac).astype(bf16).astype(jnp.float32)
        weight = jnp.where(child == index, lower, 0.0)
        weight = jnp.where(child == index + 1.0, frac, weight)
        start = pl.multiple_of(at * 32, 32)
        left_ref[pl.ds(start, 32), :] = weight.astype(bf16)
        for x in range(8):
            right_ref[pl.ds(start, 32), x * RBLOCK : (x + 1) * RBLOCK] = got_ref[
                at, x * 32 : (x + 1) * 32, :
            ]
        return carry

    lax.fori_loop(0, slots, prepare, 0)
    for half in range(0, lanes, 256):
        result = lax.dot_general(
            left_ref[:, half : half + 256], right_ref[...], (((0,), (0,)), ((), ())),
            preferred_element_type=jnp.float32,
        ).astype(bf16)
        for sub in range(256 // beams):
            w = half // beams + sub
            for x in range(8):
                out_ref[x, :, w * RBLOCK : (w + 1) * RBLOCK] = result[
                    sub * beams : (sub + 1) * beams, x * RBLOCK : (x + 1) * RBLOCK
                ]


MESH = pl.DeviceIdType.MESH
POLS = 4
RAW = 1
UNITS = POLS + RAW
RAW_FIRST = 2
LAST = POLS - 1
TAB = POLS
QUARTERS = 4
UNROLL = 16


def fused_kernel(
    tiles, shift_ref, blend_ref, foot_ref, slot_ref,
    echo_ref, replica_ref, steer_ref, phase_ref, index_ref, frac_ref, out_ref,
    ext_ref, toep_ref, big_ref, perm_ref, sub_ref, merged_ref, block_ref, kid_ref, tab_ref, wide_ref,
    kids, tabs, packed_ref, left_ref, cross_ref, part_ref, arrived_ref, own_ref,
    far_foot,
    local_sem, foot_sem, raw_send, raw_recv, halo_send, halo_recv,
    a2a_send, a2a_recv, line_send, line_recv, part_send, part_recv,
):
    g = lax.axis_index("pulse")
    t = lax.axis_index("tile")
    beams = out_ref.shape[2]
    range_dev = out_ref.shape[3]
    spans = range_dev // RBLOCK
    lanes = spans * beams
    slots = tiles * CAP
    depth = slots * 32
    pulses = echo_ref.shape[2]
    taps = replica_ref.shape[1]
    window = CBLOCK + taps
    blocks = spans

    bf16 = jnp.bfloat16
    f32 = jnp.float32
    is_mid = (g == 1) | (g == 2)
    inner = jnp.where(g == 0, 1, jnp.where(g == 1, 2, jnp.where(g == 2, 1, 2)))
    end = jnp.where(g < 2, 0, 3)
    far = 3 - end

    barrier = pltpu.get_barrier_semaphore()
    for d in range(1, tiles):
        pl.semaphore_signal(
            barrier, inc=1, device_id={"tile": lax.rem(t + d, tiles)}, device_id_type=MESH
        )
    pl.semaphore_signal(barrier, inc=1, device_id={"pulse": inner}, device_id_type=MESH)

    @pl.when(is_mid)
    def _():
        pl.semaphore_signal(barrier, inc=1, device_id={"pulse": end}, device_id_type=MESH)

    @pl.when(jnp.logical_not(is_mid))
    def _():
        pl.semaphore_signal(barrier, inc=1, device_id={"pulse": 3 - inner}, device_id_type=MESH)

    def local_copy(u):
        return pltpu.make_async_copy(
            echo_ref.at[:, u], ext_ref.at[u, :, :, pl.ds(EDGE, range_dev)], local_sem.at[u]
        )

    for u in range(POLS):
        local_copy(u).start()

    @pl.when(is_mid)
    def _():
        pl.semaphore_wait(barrier, tiles + 2)

    @pl.when(jnp.logical_not(is_mid))
    def _():
        pl.semaphore_wait(barrier, tiles)

    halos = [
        ((0, range_dev), EDGE + range_dev, -1),
        ((range_dev - EDGE, EDGE), 0, 1),
        ((0, EDGE), EDGE + 2 * range_dev, -2),
    ]

    def halo_copy(u, j, forward=False):
        (first, count), to, by = halos[j]
        if forward:
            src = ext_ref.at[u, :, :, pl.ds(EDGE + first, count)]
        else:
            src = echo_ref.at[:, u, :, pl.ds(first, count)]
        return pltpu.make_async_remote_copy(
            src_ref=src,
            dst_ref=ext_ref.at[u, :, :, pl.ds(to, count)],
            send_sem=halo_send.at[u, j], recv_sem=halo_recv.at[u, j],
            device_id={"tile": lax.rem(t + by + tiles, tiles)}, device_id_type=MESH,
        )

    def sends(j):
        by = halos[j][2]
        return (t + by >= 0) & (t + by < tiles)

    def gets(j):
        by = halos[j][2]
        return (t - by >= 0) & (t - by < tiles)

    def halo_start(u, forward=False):
        for j in range(3):
            @pl.when(sends(j))
            def _():
                halo_copy(u, j, forward).start()

    def raw_copy(i):
        return pltpu.make_async_remote_copy(
            src_ref=echo_ref.at[:, RAW_FIRST + i],
            dst_ref=ext_ref.at[POLS + i, :, :, pl.ds(EDGE, range_dev)],
            send_sem=raw_send.at[i], recv_sem=raw_recv.at[i],
            device_id={"pulse": inner}, device_id_type=MESH,
        )

    def foot_copy():
        return pltpu.make_async_remote_copy(
            src_ref=foot_ref, dst_ref=far_foot, send_sem=foot_sem.at[0], recv_sem=foot_sem.at[1],
            device_id={"pulse": inner}, device_id_type=MESH,
        )

    halo_start(0)

    @pl.when(is_mid)
    def _():
        foot_copy().start()
        for i in range(RAW):
            raw_copy(i).start()

    for u in range(UNITS):
        for j in range(3):
            (_, count), to, _ = halos[j]

            @pl.when(jnp.logical_not(gets(j)))
            def _():
                ext_ref[u, :, :, to : to + count] = jnp.zeros((2, pulses, count), bf16)

    def order_blocks(feet):
        targets = []
        for f in range(blocks):
            rank = jnp.int32(0)
            for earlier in range(f):
                rank = rank + (feet[earlier] == feet[f]).astype(jnp.int32)
            targets.append(feet[f] * CAP + rank)
        sources = []
        for s in range(slots):
            source = jnp.int32(0)
            for f in range(blocks):
                source = source + f * (targets[f] == s).astype(jnp.int32)
            sources.append(source)
        return sources

    @pl.when(jnp.logical_not(is_mid))
    def _():
        for f in range(blocks):
            far_foot[0, f] = jnp.int32(0)

    sources = order_blocks([foot_ref[0, f] for f in range(blocks)])
    tab_row = iota((TABROWS, RBLOCK), 0)
    for f in range(blocks):
        index_f = index_ref[0, f : f + 1, :].astype(f32)
        frac_f = frac_ref[0, f : f + 1, :].astype(f32)
        landing = (slot_ref[0, f] + 1).astype(f32)
        table = jnp.where(tab_row == 0, index_f, jnp.where(tab_row == 1, frac_f, 0.0))
        wide_ref[f] = jnp.where(tab_row == 2, landing, table).astype(bf16)
    for s in range(slots):
        tab_ref[s] = wide_ref[sources[s]]

    def tab_copy(d, peer, place):
        return pltpu.make_async_remote_copy(
            src_ref=tab_ref.at[pl.ds(peer * CAP, CAP)],
            dst_ref=tabs.at[pl.ds(place * CAP, CAP)],
            send_sem=a2a_send.at[UNITS, d - 1], recv_sem=a2a_recv.at[UNITS, d - 1],
            device_id={"tile": peer}, device_id_type=MESH,
        )

    def unit_place(u):
        return jnp.where(u < POLS, g, inner), jnp.where(u < POLS, u, u - POLS + RAW_FIRST)

    def spread_copy(u, d, peer, place):
        group, pol = unit_place(u)
        return pltpu.make_async_remote_copy(
            src_ref=kid_ref.at[u, :, pl.ds(peer * CAP, CAP)],
            dst_ref=kids.at[group, pol, :, pl.ds(place * CAP, CAP)],
            send_sem=a2a_send.at[u, d - 1], recv_sem=a2a_recv.at[u, d - 1],
            device_id={"tile": peer}, device_id_type=MESH,
        )

    def spread_start(u):
        for d in range(1, tiles):
            spread_copy(u, d, lax.rem(t + d, tiles), t).start()
        group, pol = unit_place(u)
        kids[group, pol, :, pl.ds(t * CAP, CAP)] = kid_ref[u, :, pl.ds(t * CAP, CAP)]

    def spread_wait(u):
        for d in range(1, tiles):
            peer = lax.rem(t + tiles - d, tiles)
            spread_copy(u, d, peer, peer).wait_recv()

    def line_copy(k, group, lane, to):
        part = kids.at[group, k]
        return pltpu.make_async_remote_copy(
            src_ref=part, dst_ref=part,
            send_sem=line_send.at[lane, k], recv_sem=line_recv.at[group, k],
            device_id={"pulse": to}, device_id_type=MESH,
        )

    def line_tab(group, lane, to):
        part = packed_ref.at[group]
        return pltpu.make_async_remote_copy(
            src_ref=part, dst_ref=part,
            send_sem=line_send.at[lane, TAB], recv_sem=line_recv.at[group, TAB],
            device_id={"pulse": to}, device_id_type=MESH,
        )

    for d in range(1, tiles):
        tab_copy(d, lax.rem(t + d, tiles), t).start()
    tabs[pl.ds(t * CAP, CAP)] = tab_ref[pl.ds(t * CAP, CAP)]

    for part in range(2):
        line = replica_ref[part : part + 1, :].astype(f32)
        line = jnp.concatenate([line, jnp.zeros((1, CBLOCK), f32)], axis=1)
        rolled = pltpu.roll(
            jnp.broadcast_to(line, (CBLOCK, window)), 0, 1, stride=1, stride_axis=0
        )
        if part == 0:
            toep_ref[0:CBLOCK, 0:window] = rolled.astype(bf16)
            toep_ref[CBLOCK:, window:] = rolled.astype(bf16)
        else:
            toep_ref[0:CBLOCK, window:] = rolled.astype(bf16)
            toep_ref[CBLOCK:, 0:window] = (-rolled).astype(bf16)

    halo_start(1)

    row = iota((64, 16), 0)
    angle = jnp.zeros((64, 16), f32)
    for a in range(16):
        angle = jnp.where(((row >> 1) & 15) == a, steer_ref[a : a + 1, :], angle)
    on_row = iota((32, 32), 0) == iota((32, 32), 1)
    turns = [
        jnp.sum(jnp.where(on_row, phase_ref[c : c + 1, :], 0.0), axis=1, keepdims=True)
        for c in range(2)
    ]
    angle = angle + jnp.concatenate(turns, axis=0)
    scale = math.sqrt(0.5) / math.sqrt(steer_ref.shape[1])
    cosine, sine = jnp.cos(angle) * scale, jnp.sin(angle) * scale
    small = jnp.concatenate(
        [
            jnp.concatenate([cosine, -sine], axis=1),
            jnp.concatenate([sine, cosine], axis=1),
        ],
        axis=0,
    ).astype(bf16)
    o_at = iota((512, 128), 0)
    tall = ((o_at & 1) * 64 + (o_at >> 3) == iota((512, 128), 1)).astype(bf16)
    i_at = iota((32, 256), 1)
    broad = (((i_at >> 5) & 1) * 16 + (i_at & 15) == iota((32, 256), 0)).astype(bf16)
    spread = jnp.dot(tall, small, preferred_element_type=f32).astype(bf16)
    spread = jnp.dot(spread, broad, preferred_element_type=f32)
    o_all, i_all = iota((512, 256), 0), iota((512, 256), 1)
    same = (((o_all >> 1) & 3) == (i_all >> 6)) & ((o_all >> 8) == ((i_all >> 4) & 1))
    big_ref[...] = jnp.where(same, spread, 0.0).astype(bf16)
    o_all, i_all = iota((256, 256), 0), iota((256, 256), 1)
    order_in = (o_all & 31) * 8 + ((o_all >> 5) & 3) * 2 + (o_all >> 7)
    perm_ref[...] = (i_all == order_in).astype(bf16)

    @pl.when(is_mid)
    def _():
        foot_copy().wait_recv()

    far_sources = order_blocks([far_foot[0, f] for f in range(blocks)])

    def begin_tab():
        for d in range(1, tiles):
            peer = lax.rem(t + tiles - d, tiles)
            tab_copy(d, peer, peer).wait_recv()
        row, column = iota((3 * slots, slots * TABROWS), 0), iota((3 * slots, slots * TABROWS), 1)
        choose = column == (row & (slots - 1)) * TABROWS + row // slots
        packed_ref[g] = jnp.dot(
            choose.astype(bf16), tabs[...].reshape(slots * TABROWS, RBLOCK),
            preferred_element_type=f32,
        ).astype(bf16)
        line_tab(g, 0, inner).start()

    def relay(k):
        line_copy(k, end, 0, inner).wait_recv()
        line_copy(k, end, 1, inner).start()

    def form(u):
        @pl.when(u < POLS)
        def _():
            local_copy(u).wait()

        for j in range(3):
            @pl.when(gets(j))
            def _():
                halo_copy(u, j, True).wait_recv()

        pieces = []
        for j in range(9):
            start = j * CBLOCK
            pieces.append(
                jnp.concatenate(
                    [ext_ref[u, 0, :, start : start + window], ext_ref[u, 1, :, start : start + window]],
                    axis=1,
                )
            )
        found = lax.dot_general(
            jnp.concatenate(pieces, axis=0), toep_ref[...], (((1,), (1,)), ((), ())),
            preferred_element_type=f32,
        ).astype(bf16)
        before = (iota((pulses, 2 * CBLOCK), 1) & (CBLOCK - 1)) < EDGE
        first = jnp.where(before & (t == 0), 0.0, found[0:pulses].astype(f32)).astype(bf16)
        for jj in range(3):
            stacked = []
            for q in range(QUARTERS):
                at = 2 * q + jj
                one = first if at == 0 else found[at * pulses : (at + 1) * pulses]
                stacked += [one[:, :CBLOCK], one[:, CBLOCK:]]
            sub_ref[:, jj * CBLOCK : (jj + 1) * CBLOCK] = jnp.dot(
                big_ref[...], jnp.concatenate(stacked, axis=0), preferred_element_type=f32
            )

        def merge(b, carry):
            totals = [None] * 4
            for c in range(2):
                by = shift_ref[c, b]
                weight = blend_ref[c, b]
                back = by < 0
                turn = jnp.where(back, by + RBLOCK, by)
                x = sub_ref[pl.ds(pl.multiple_of((c * 32 + b) * 8, 8), 8), :]
                x = jnp.concatenate([x[:, i * RBLOCK : (i + 1) * RBLOCK] for i in range(6)], axis=0)
                x = jnp.where(back, x[:40], x[8:])
                low = pltpu.roll(x, (RBLOCK - turn) & (RBLOCK - 1), 1)
                high = pltpu.roll(x, RBLOCK - 1 - turn, 1)
                lane = iota((32, RBLOCK), 1)
                low = jnp.where(lane < RBLOCK - turn, low[:32], low[8:])
                high = jnp.where(lane < RBLOCK - 1 - turn, high[:32], high[8:])
                y = (1.0 - weight) * low + weight * high
                totals = y if c == 0 else totals + y
            for i in range(4):
                merged_ref[pl.ds(pl.multiple_of(b * 8, 8), 8), i * RBLOCK : (i + 1) * RBLOCK] = (
                    totals[i * 8 : (i + 1) * 8]
                )
            return carry

        lax.fori_loop(0, 32, merge, 0, unroll=UNROLL)
        ordered = jnp.dot(
            perm_ref[...], merged_ref[...].astype(bf16), preferred_element_type=f32
        ).astype(bf16)
        for part in range(2):
            for f in range(blocks):
                at = (part * QUARTERS + f // 4) * 32
                block_ref[f, part] = ordered[at : at + 32, (f % 4) * RBLOCK : (f % 4 + 1) * RBLOCK]
        for s in range(slots):
            kid_ref[u, :, s] = block_ref[jnp.where(u < POLS, sources[s], far_sources[s])]
        spread_start(u)

    def own_line(k):
        spread_wait(k)
        line_copy(k, g, 0, inner).start()

    def forward(i):
        raw_copy(i).wait_recv()
        halo_start(POLS + i, True)

    middle = spans // 2 * RBLOCK

    def part_copy(k, half, to, place):
        span = pl.ds(half * middle, middle)
        return pltpu.make_async_remote_copy(
            src_ref=part_ref.at[k, :, :, span], dst_ref=arrived_ref.at[place, :, :, span],
            send_sem=part_send.at[k, half], recv_sem=part_recv.at[place, half],
            device_id={"pulse": to}, device_id_type=MESH,
        )

    def prepare(ref, group, beam_group, row, column, used):
        expand = (
            (iota((RBLOCK, lanes), 1) & (beams - 1)) + beam_group * beams
            == iota((RBLOCK, lanes), 0)
        ).astype(bf16)
        where_at = (iota((1, lanes), 1) // beams + 1).astype(f32)
        child = iota((32, lanes), 0).astype(f32)

        wide = jnp.dot(packed_ref[group], expand, preferred_element_type=f32)
        for at in range(slots // 4):
            pieces = []
            for slot in range(at * 4, at * 4 + 4):
                landing = wide[2 * slots + slot : 2 * slots + slot + 1, :]
                index = jnp.where(
                    (landing == where_at) & used, wide[slot : slot + 1, :], -9.0
                )
                frac = wide[slots + slot : slots + slot + 1, :]
                lower = (1.0 - frac).astype(bf16).astype(f32)
                weight = jnp.where(child == index, lower, 0.0)
                pieces.append(jnp.where(child == index + 1.0, frac, weight))
            block = jnp.concatenate(pieces, axis=0)
            at_column = pl.multiple_of(column + at * 128, 128)
            ref[row : row + lanes, pl.ds(at_column, 128)] = block.T.astype(bf16)

    def put(ref, k, half, result):
        for step in range(spans // 2):
            w = half * (spans // 2) + step
            for i in range(2):
                ref[k, i, :, w * RBLOCK : (w + 1) * RBLOCK] = result[
                    step * beams : (step + 1) * beams, i * RBLOCK : (i + 1) * RBLOCK
                ]

    side = jnp.where(g < 2, 0, 2)

    def prepare_all():
        line_tab(inner, 0, inner).wait_recv()
        line_tab(far, 0, inner).wait_recv()

        def prepare_group(group, carry):
            column = pl.multiple_of(group * depth, 128)
            prepare(left_ref, group, g, 0, column, group >= 0)
            prepare(left_ref, group, end, lanes, column, group != end)
            return carry

        lax.fori_loop(0, 4, prepare_group, 0)

        def prepare_cross(at, carry):
            column = pl.multiple_of(at * depth, 128)
            prepare(cross_ref, side + at, far, 0, column, at >= 0)
            prepare(cross_ref, side + at, inner, lanes, column, at >= 0)
            return carry

        lax.fori_loop(0, 2, prepare_cross, 0)

    def final(k):
        line_copy(k, far, 0, inner).wait_recv()
        right = jnp.concatenate(
            [kids[:, k, i].reshape(4 * depth, RBLOCK) for i in range(2)], axis=1
        )
        for half in range(2):
            first = lanes + half * (lanes // 2)
            put(part_ref, k, half, jnp.dot(
                left_ref[first : first + lanes // 2, :], right, preferred_element_type=f32
            ).astype(bf16))
            part_copy(k, half, end, k).start()
        for half in range(2):
            first = half * (lanes // 2)
            result = jnp.dot(
                left_ref[first : first + lanes // 2, :], right, preferred_element_type=f32
            ).astype(bf16)
            for step in range(spans // 2):
                w = half * (spans // 2) + step
                for i in range(2):
                    out_ref[i, k, :, w * RBLOCK : (w + 1) * RBLOCK] = result[
                        step * beams : (step + 1) * beams, i * RBLOCK : (i + 1) * RBLOCK
                    ]

    def cross():
        line_copy(LAST, end, 0, inner).wait_recv()
        right = jnp.concatenate(
            [kids[pl.ds(side, 2), LAST, i].reshape(2 * depth, RBLOCK) for i in range(2)], axis=1
        )
        for at in range(2):
            for half in range(2):
                first = at * lanes + half * (lanes // 2)
                put(part_ref, POLS + at, half, jnp.dot(
                    cross_ref[first : first + lanes // 2, :], right, preferred_element_type=f32
                ).astype(bf16))
                part_copy(POLS + at, half, inner if at else far, POLS).start()
        columns = pl.ds(pl.multiple_of(side * depth, 128), 2 * depth)
        for half in range(2):
            first = half * (lanes // 2)
            put(own_ref, LAST, half, jnp.dot(
                left_ref[first : first + lanes // 2, columns], right, preferred_element_type=f32
            ))

    def last_part():
        right = jnp.concatenate(
            [kids[g, LAST, i].reshape(depth, RBLOCK) for i in range(2)], axis=1
        )
        columns = pl.ds(pl.multiple_of(g * depth, 128), depth)
        for half in range(2):
            first = lanes + half * (lanes // 2)
            put(part_ref, LAST, half, jnp.dot(
                left_ref[first : first + lanes // 2, columns], right, preferred_element_type=f32
            ).astype(bf16))
            part_copy(LAST, half, end, LAST).start()

    def mid_unit(u):
        return jnp.where(u == 2, 3, jnp.where(u == 3, 2, u))

    def step(i, carry):
        @pl.when(is_mid & (i == 4))
        def _():
            prepare_all()
            spread_wait(LAST)
            last_part()

        form(jnp.where(is_mid, mid_unit(i), i))

        @pl.when(i == 0)
        def _():
            begin_tab()

        @pl.when(is_mid & (i < 2))
        def _():
            halo_start(3 - i)

        @pl.when(jnp.logical_not(is_mid) & (i + 2 < POLS))
        def _():
            halo_start(i + 2)

        @pl.when(jnp.logical_not(is_mid) & (i >= 1))
        def _():
            own_line(i - 1)

        @pl.when(is_mid & (i == 1))
        def _():
            forward(0)
            own_line(0)

        @pl.when(is_mid & (i == 2))
        def _():
            own_line(1)
            line_tab(end, 0, inner).wait_recv()
            line_tab(end, 1, inner).start()

        @pl.when(is_mid & (i == 3))
        def _():
            relay(0)

        return carry

        return carry

    units = jnp.where(is_mid, UNITS, POLS)
    lax.fori_loop(0, units, step, 0)

    @pl.when(is_mid)
    def _():
        relay(1)

        def later(k, carry):
            @pl.when(k < RAW_FIRST)
            def _():
                line_copy(k, inner, 0, inner).wait_recv()

            @pl.when(k == RAW_FIRST)
            def _():
                cross()
                spread_wait(RAW_FIRST)
                spread_wait(POLS)

            final(k)

            @pl.when(k == 0)
            def _():
                relay(2)

            return carry

        lax.fori_loop(0, LAST, later, 0)
        for half in range(2):
            part_copy(POLS + 1, half, inner, POLS).wait_recv()
            span = slice(half * middle, (half + 1) * middle)
            for i in range(2):
                out_ref[i, LAST, :, span] = (
                    own_ref[LAST, i, :, span] + arrived_ref[POLS, i, :, span].astype(f32)
                ).astype(bf16)
        line_tab(g, 0, inner).wait_send()
        line_tab(end, 1, inner).wait_send()
        for k in range(RAW_FIRST):
            line_copy(k, g, 0, inner).wait_send()
        for k in range(LAST):
            line_copy(k, end, 1, inner).wait_send()
        for half in range(2):
            for k in range(POLS):
                part_copy(k, half, end, k).wait_send()
            part_copy(POLS, half, far, POLS).wait_send()
            part_copy(POLS + 1, half, inner, POLS).wait_send()
        foot_copy().wait_send()
        for i in range(RAW):
            raw_copy(i).wait_send()

    @pl.when(jnp.logical_not(is_mid))
    def _():
        own_line(LAST)
        prepare(left_ref, g, g, 0, 0, g >= 0)

        def product(k, carry):
            right = jnp.concatenate(
                [kids[g, k, i].reshape(depth, RBLOCK) for i in range(2)], axis=1
            )
            for half in range(2):
                first = half * (lanes // 2)
                put(own_ref, k, half, jnp.dot(
                    left_ref[first : first + lanes // 2, :depth], right,
                    preferred_element_type=f32,
                ))
            return carry

        lax.fori_loop(0, POLS, product, 0)

        def finish(k, carry):
            for half in range(2):
                part_copy(k, half, inner, k).wait_recv()
                span = slice(half * middle, (half + 1) * middle)
                for i in range(2):
                    out_ref[i, k, :, span] = (
                        own_ref[k, i, :, span] + arrived_ref[k, i, :, span].astype(f32)
                    ).astype(bf16)
            return carry

        lax.fori_loop(0, LAST, finish, 0)
        for half in range(2):
            part_copy(LAST, half, inner, LAST).wait_recv()
            part_copy(POLS, half, inner, POLS).wait_recv()
            span = slice(half * middle, (half + 1) * middle)
            for i in range(2):
                out_ref[i, LAST, :, span] = (
                    own_ref[LAST, i, :, span]
                    + arrived_ref[LAST, i, :, span].astype(f32)
                    + arrived_ref[POLS, i, :, span].astype(f32)
                ).astype(bf16)
        line_tab(g, 0, inner).wait_send()
        for k in range(POLS):
            line_copy(k, g, 0, inner).wait_send()

    for d in range(1, tiles):
        tab_copy(d, lax.rem(t + d, tiles), t).wait_send()

    def drain(u, carry):
        for d in range(1, tiles):
            spread_copy(u, d, lax.rem(t + d, tiles), t).wait_send()
        for j in range(3):
            @pl.when(sends(j))
            def _():
                halo_copy(u, j, True).wait_send()
        return carry

    lax.fori_loop(0, units, drain, 0)


def fused(
    shift, blend, foot, slot, echoes, replica, steer_phase, merge_phase, index, frac,
    tiles, beams, range_dev,
):
    slots = tiles * CAP
    lanes = range_dev // RBLOCK * beams
    bf16 = jnp.bfloat16
    f32 = jnp.float32
    pulses = echoes.shape[2]
    vmem = pl.BlockSpec(memory_space=pltpu.VMEM)
    smem = pl.BlockSpec(memory_space=pltpu.SMEM)
    dma = pltpu.SemaphoreType.DMA
    return pl.pallas_call(
        functools.partial(fused_kernel, tiles),
        out_shape=jax.ShapeDtypeStruct((2, POLS, beams, range_dev), bf16),
        in_specs=[smem] * 4 + [pl.BlockSpec(memory_space=pl.ANY)] + [vmem] * 5,
        out_specs=vmem,
        scratch_shapes=[
            pltpu.VMEM((UNITS, 2, pulses, 2 * range_dev + 2 * EDGE), bf16),
            pltpu.VMEM((2 * CBLOCK, 2 * (CBLOCK + replica.shape[1])), bf16),
            pltpu.VMEM((512, 256), bf16),
            pltpu.VMEM((256, 256), bf16),
            pltpu.VMEM((512, 3 * CBLOCK), f32),
            pltpu.VMEM((256, 4 * RBLOCK), f32),
            pltpu.VMEM((slots, 2, 32, RBLOCK), bf16),
            pltpu.VMEM((UNITS, 2, slots, 32, RBLOCK), bf16),
            pltpu.VMEM((slots, TABROWS, RBLOCK), bf16),
            pltpu.VMEM((slots, TABROWS, RBLOCK), bf16),
            pltpu.VMEM((4, POLS, 2, slots, 32, RBLOCK), bf16),
            pltpu.VMEM((slots, TABROWS, RBLOCK), bf16),
            pltpu.VMEM((4, 3 * slots, RBLOCK), bf16),
            pltpu.VMEM((2 * lanes, 4 * slots * 32), bf16),
            pltpu.VMEM((2 * lanes, 2 * slots * 32), bf16),
            pltpu.VMEM((POLS + 2, 2, beams, range_dev), bf16),
            pltpu.VMEM((POLS + 1, 2, beams, range_dev), bf16),
            pltpu.VMEM((POLS, 2, beams, range_dev), f32),
            pltpu.SMEM((1, range_dev // RBLOCK), jnp.int32),
            dma((POLS,)),
            dma((2,)),
            dma((RAW,)),
            dma((RAW,)),
            dma((UNITS, 3)),
            dma((UNITS, 3)),
            dma((UNITS + 1, tiles - 1)),
            dma((UNITS + 1, tiles - 1)),
            dma((2, POLS + 1)),
            dma((4, POLS + 1)),
            dma((POLS + 2, 2)),
            dma((POLS + 1, 2)),
        ],
        compiler_params=pltpu.CompilerParams(
            collective_id=0, has_side_effects=True, vmem_limit_bytes=40 << 20
        ),
    )(shift, blend, foot, slot, echoes, replica, steer_phase, merge_phase, index, frac)


def shards(
    echoes, replica, steer_phase, range_shift, merge_phase, merge_frac,
    footprint, row_slot, beam_index, beam_frac,
):
    pulse_count, pol_count, range_dev = echoes.shape[1:]
    rows = pulse_count * pol_count
    taps = replica.shape[1]
    final_beams = beam_index.shape[2]
    tiles = lax.axis_size("tile")
    groups = lax.axis_size("pulse")
    slot_count = tiles * CAP
    scale = 1.0 / math.sqrt(steer_phase.shape[1])
    steer_re = jnp.cos(steer_phase) * scale
    steer_im = jnp.sin(steer_phase) * scale
    steer = jnp.concatenate(
        [
            jnp.concatenate([steer_re, -steer_im], axis=1),
            jnp.concatenate([steer_im, steer_re], axis=1),
        ],
        axis=0,
    ).astype(jnp.bfloat16)
    half_root = math.sqrt(0.5)
    coef = jnp.stack(
        [
            merge_frac.reshape(-1),
            (jnp.cos(merge_phase) * half_root).reshape(-1),
            (jnp.sin(merge_phase) * half_root).reshape(-1),
        ]
    )
    beams = final_beams // groups
    if groups == 4 and slot_count == range_dev // RBLOCK:
        return fused(
            range_shift, merge_frac, footprint, row_slot, echoes.transpose(0, 2, 1, 3),
            replica, steer_phase, merge_phase, beam_index, beam_frac, tiles, beams, range_dev,
        )
    own = echoes.reshape(2, rows, range_dev)
    following = shifted(own, "tile", -1)
    before = shifted(own[:, :, range_dev - EDGE :], "tile", 1)
    after = shifted(own[:, :, :EDGE], "tile", -2)

    width = range_dev + CBLOCK
    smem = pl.BlockSpec(memory_space=pltpu.SMEM)
    vmem = pl.BlockSpec(memory_space=pltpu.VMEM)
    kids, tabs = pl.pallas_call(
        form_kernel,
        out_shape=(
            jax.ShapeDtypeStruct((8, slot_count, 32, RBLOCK), jnp.bfloat16),
            jax.ShapeDtypeStruct((slot_count, TABROWS, RBLOCK), jnp.bfloat16),
        ),
        in_specs=[smem] * 4 + [vmem] * 8,
        out_specs=(vmem, vmem),
        scratch_shapes=[
            pltpu.VMEM((2, rows, 2 * range_dev + 2 * EDGE), jnp.bfloat16),
            pltpu.VMEM((2 * CBLOCK, 2 * (CBLOCK + taps)), jnp.bfloat16),
            pltpu.VMEM((256, width), jnp.float32),
            pltpu.VMEM((256, range_dev), jnp.bfloat16),
        ],
        compiler_params=pltpu.CompilerParams(vmem_limit_bytes=56 << 20),
    )(
        range_shift, coef, footprint, row_slot,
        own, following, before, after, replica, steer, beam_index, beam_frac,
    )
    sent = jnp.concatenate(
        [kids.transpose(1, 0, 2, 3).reshape(slot_count, 256, RBLOCK), tabs], axis=1
    )
    got = lax.all_to_all(
        sent.reshape(tiles, CAP, 256 + TABROWS, RBLOCK), "tile",
        split_axis=0, concat_axis=0, tiled=True,
    ).reshape(slot_count, 256 + TABROWS, RBLOCK)
    gathered = lax.all_gather(got, "pulse", axis=0, tiled=True)
    total_slots = groups * slot_count
    image = pl.pallas_call(
        place_kernel,
        out_shape=jax.ShapeDtypeStruct((2 * pol_count, beams, range_dev), jnp.bfloat16),
        in_specs=[vmem],
        out_specs=vmem,
        scratch_shapes=[
            pltpu.VMEM((total_slots * 32, range_dev // RBLOCK * beams), jnp.bfloat16),
            pltpu.VMEM((total_slots * 32, 8 * RBLOCK), jnp.bfloat16),
        ],
        compiler_params=pltpu.CompilerParams(vmem_limit_bytes=56 << 20),
    )(gathered)
    return image.reshape(2, pol_count, beams, range_dev)


def solution(mesh):
    placed = (
        P(None, "pulse", None, "tile"),
        P(),
        P(),
        P(),
        P(),
        P(),
        P("pulse", "tile"),
        P("pulse", "tile"),
        P("pulse", "tile", None),
        P("pulse", "tile", None),
    )
    return jax.shard_map(
        shards,
        mesh=mesh,
        in_specs=placed,
        out_specs=P(None, None, "pulse", "tile"),
        check_vma=False,
    )
```

```python
import functools
import math

import jax
import jax.numpy as jnp
from jax import lax
from jax.experimental import pallas as pl
from jax.experimental.pallas import tpu as pltpu
from jax.sharding import PartitionSpec as P

RBLOCK = 128
CAP = 2
CBLOCK = 256
EDGE = 128
TABROWS = 16


def shifted(value, axis, by):
    count = lax.axis_size(axis)
    pairs = [(i, i + by) for i in range(count) if 0 <= i + by < count]
    return lax.ppermute(value, axis, pairs)


def iota(shape, dim):
    return lax.broadcasted_iota(jnp.int32, shape, dim)


def form_kernel(
    shift_ref, coef_ref, foot_ref, slot_ref,
    own_ref, next_ref, prev_ref, after_ref, replica_ref, steer_ref, index_ref, frac_ref,
    kid_ref, tab_ref,
    ext_ref, toep_ref, sub_ref, merged_ref,
):
    range_dev = own_ref.shape[2]
    rows = own_ref.shape[1]
    taps = replica_ref.shape[1]
    window = CBLOCK + taps
    width = sub_ref.shape[1]
    blocks = range_dev // RBLOCK
    bf16 = jnp.bfloat16

    ext_ref[:, :, 0:EDGE] = prev_ref[...]
    ext_ref[:, :, EDGE : EDGE + range_dev] = own_ref[...]
    ext_ref[:, :, EDGE + range_dev : EDGE + 2 * range_dev] = next_ref[...]
    ext_ref[:, :, EDGE + 2 * range_dev :] = after_ref[...]

    for part in range(2):
        line = replica_ref[part : part + 1, :].astype(jnp.float32)
        line = jnp.concatenate([line, jnp.zeros((1, CBLOCK), jnp.float32)], axis=1)
        rolled = pltpu.roll(
            jnp.broadcast_to(line, (CBLOCK, window)), 0, 1, stride=1, stride_axis=0
        )
        if part == 0:
            toep_ref[0:CBLOCK, 0:window] = rolled.astype(bf16)
            toep_ref[CBLOCK:, window:] = rolled.astype(bf16)
        else:
            toep_ref[0:CBLOCK, window:] = rolled.astype(bf16)
            toep_ref[CBLOCK:, 0:window] = (-rolled).astype(bf16)

    r_at = iota((256, 32), 0)
    left = (((r_at >> 2) & 1) * 16 + ((r_at >> 3) & 15) == iota((256, 32), 1)).astype(bf16)
    k_at = iota((32, 256), 1)
    right = ((k_at >> 7) * 16 + ((k_at >> 2) & 15) == iota((32, 256), 0)).astype(bf16)
    spread = jnp.dot(left, steer_ref[...], preferred_element_type=jnp.float32).astype(bf16)
    spread = jnp.dot(spread, right, preferred_element_type=jnp.float32)
    r_all, k_all = iota((256, 256), 0), iota((256, 256), 1)
    same = ((r_all >> 7) == ((k_all >> 6) & 1)) & ((r_all & 3) == (k_all & 3))
    steer = jnp.where(same, spread, 0.0).astype(bf16)

    group = 3

    def compress(at, carry):
        pieces = []
        for step in range(group):
            start = pl.multiple_of((at * group + step) * CBLOCK, CBLOCK)
            pieces.append(
                jnp.concatenate(
                    [ext_ref[0, :, pl.ds(start, window)], ext_ref[1, :, pl.ds(start, window)]],
                    axis=1,
                )
            )
        left_side = jnp.concatenate(pieces, axis=0)
        found = lax.dot_general(
            left_side, toep_ref[...], (((1,), (1,)), ((), ())),
            preferred_element_type=jnp.float32,
        ).astype(bf16)
        for step in range(group):
            start = pl.multiple_of((at * group + step) * CBLOCK, CBLOCK)
            one = found[step * rows : (step + 1) * rows]
            stacked = jnp.concatenate([one[:, :CBLOCK], one[:, CBLOCK:]], axis=0)
            sub = jnp.dot(steer, stacked, preferred_element_type=jnp.float32)
            sub_ref[:, pl.ds(start, CBLOCK)] = sub.astype(bf16).astype(jnp.float32)
        return carry

    lax.fori_loop(0, width // (CBLOCK * group), compress, 0)

    @pl.when(lax.axis_index("tile") == 0)
    def _():
        sub_ref[:, 0:EDGE] = jnp.zeros((256, EDGE), jnp.float32)

    sign = jnp.where(iota((8, width), 0) < 4, -1.0, 1.0).astype(jnp.float32)

    def merge(a, carry):
        totals = [None, None]
        for c in range(2):
            x = sub_ref[pl.ds(pl.multiple_of((c * 16 + a) * 8, 8), 8), :]
            x_up = pltpu.roll(x, width - 1, 1)
            for parity in range(2):
                b = 2 * a + parity
                weight = coef_ref[0, c * 32 + b]
                cosine = coef_ref[1, c * 32 + b]
                sine = coef_ref[2, c * 32 + b]
                y = (1.0 - weight) * x + weight * x_up
                v = cosine * y + (sine * sign) * pltpu.roll(y, 4, 0)
                by = shift_ref[c, b]
                z = pltpu.roll(v, jnp.where(by > 0, width - by, -by), 1)
                z = z[:, EDGE : EDGE + range_dev]
                totals[parity] = z if totals[parity] is None else totals[parity] + z
        merged_ref[pl.ds(pl.multiple_of(a * 16, 16), 16), :] = jnp.concatenate(
            totals, axis=0
        ).astype(bf16)
        return carry

    lax.fori_loop(0, 16, merge, 0)

    order = (k_all == (r_all & 31) * 8 + (r_all >> 5)).astype(bf16)
    if tab_ref.shape[0] > blocks:
        kid_ref[...] = jnp.zeros(kid_ref.shape, bf16)
        tab_ref[...] = jnp.zeros(tab_ref.shape, bf16)
    tab_row = iota((TABROWS, RBLOCK), 0)
    for f in range(blocks):
        foot = foot_ref[0, f]
        rank = jnp.int32(0)
        for before in range(f):
            rank = rank + (foot_ref[0, before] == foot).astype(jnp.int32)
        slot = foot * CAP + rank
        part = jnp.dot(
            order, merged_ref[:, f * RBLOCK : (f + 1) * RBLOCK],
            preferred_element_type=jnp.float32,
        )
        kid_ref[:, slot] = part.astype(bf16).reshape(8, 32, RBLOCK)
        landing = (slot_ref[0, f] + 1).astype(jnp.float32)
        index_f = index_ref[0, f : f + 1, :].astype(jnp.float32)
        frac_f = frac_ref[0, f : f + 1, :].astype(jnp.float32)
        table = jnp.where(tab_row == 0, index_f, jnp.where(tab_row == 1, frac_f, 0.0))
        table = jnp.where(tab_row == 2, landing, table)
        tab_ref[slot] = table.astype(bf16)


def place_kernel(got_ref, out_ref, left_ref, right_ref):
    slots = got_ref.shape[0]
    beams = out_ref.shape[1]
    spans = out_ref.shape[2] // RBLOCK
    lanes = spans * beams
    mine = lax.axis_index("pulse") * beams
    bf16 = jnp.bfloat16
    lane = iota((RBLOCK, lanes), 1)
    widen = ((lane & (beams - 1)) + mine == iota((RBLOCK, lanes), 0)).astype(bf16)
    where_at = iota((1, lanes), 1) // beams + 1
    child = iota((32, lanes), 0).astype(jnp.float32)

    def prepare(at, carry):
        table = got_ref[at, 256 : 256 + TABROWS, :]
        wide = jnp.dot(table, widen, preferred_element_type=jnp.float32)
        landing = wide[2:3, :]
        index = jnp.where(landing == where_at.astype(jnp.float32), wide[0:1, :], -9.0)
        frac = wide[1:2, :]
        lower = (1.0 - frac).astype(bf16).astype(jnp.float32)
        weight = jnp.where(child == index, lower, 0.0)
        weight = jnp.where(child == index + 1.0, frac, weight)
        start = pl.multiple_of(at * 32, 32)
        left_ref[pl.ds(start, 32), :] = weight.astype(bf16)
        for x in range(8):
            right_ref[pl.ds(start, 32), x * RBLOCK : (x + 1) * RBLOCK] = got_ref[
                at, x * 32 : (x + 1) * 32, :
            ]
        return carry

    lax.fori_loop(0, slots, prepare, 0)
    for half in range(0, lanes, 256):
        result = lax.dot_general(
            left_ref[:, half : half + 256], right_ref[...], (((0,), (0,)), ((), ())),
            preferred_element_type=jnp.float32,
        ).astype(bf16)
        for sub in range(256 // beams):
            w = half // beams + sub
            for x in range(8):
                out_ref[x, :, w * RBLOCK : (w + 1) * RBLOCK] = result[
                    sub * beams : (sub + 1) * beams, x * RBLOCK : (x + 1) * RBLOCK
                ]


MESH = pl.DeviceIdType.MESH
POLS = 4
RAW = 2
UNITS = POLS + RAW
RAW_FIRST = 1
LAST = POLS - 1
TAB = POLS
QUARTERS = 4
UNROLL = 16


def fused_kernel(
    tiles, shift_ref, blend_ref, foot_ref, slot_ref,
    echo_ref, replica_ref, steer_ref, phase_ref, index_ref, frac_ref, out_ref,
    ext_ref, toep_ref, big_ref, perm_ref, sub_ref, merged_ref, block_ref, kid_ref, tab_ref, wide_ref,
    kids, tabs, packed_ref, left_ref, cross_ref, part_ref, arrived_ref, own_ref,
    far_foot,
    local_sem, foot_sem, raw_send, raw_recv, halo_send, halo_recv,
    a2a_send, a2a_recv, line_send, line_recv, part_send, part_recv,
):
    g = lax.axis_index("pulse")
    t = lax.axis_index("tile")
    beams = out_ref.shape[2]
    range_dev = out_ref.shape[3]
    spans = range_dev // RBLOCK
    lanes = spans * beams
    slots = tiles * CAP
    depth = slots * 32
    pulses = echo_ref.shape[2]
    taps = replica_ref.shape[1]
    window = CBLOCK + taps
    blocks = spans

    bf16 = jnp.bfloat16
    f32 = jnp.float32
    is_mid = (g == 1) | (g == 2)
    inner = jnp.where(g == 0, 1, jnp.where(g == 1, 2, jnp.where(g == 2, 1, 2)))
    end = jnp.where(g < 2, 0, 3)
    far = 3 - end

    barrier = pltpu.get_barrier_semaphore()
    for d in range(1, tiles):
        pl.semaphore_signal(
            barrier, inc=1, device_id={"tile": lax.rem(t + d, tiles)}, device_id_type=MESH
        )
    pl.semaphore_signal(barrier, inc=1, device_id={"pulse": inner}, device_id_type=MESH)

    @pl.when(is_mid)
    def _():
        pl.semaphore_signal(barrier, inc=1, device_id={"pulse": end}, device_id_type=MESH)

    @pl.when(jnp.logical_not(is_mid))
    def _():
        pl.semaphore_signal(barrier, inc=1, device_id={"pulse": 3 - inner}, device_id_type=MESH)

    def local_copy(u):
        return pltpu.make_async_copy(
            echo_ref.at[:, u], ext_ref.at[u, :, :, pl.ds(EDGE, range_dev)], local_sem.at[u]
        )

    for u in range(POLS):
        local_copy(u).start()

    @pl.when(is_mid)
    def _():
        pl.semaphore_wait(barrier, tiles + 2)

    @pl.when(jnp.logical_not(is_mid))
    def _():
        pl.semaphore_wait(barrier, tiles)

    halos = [
        ((0, range_dev), EDGE + range_dev, -1),
        ((range_dev - EDGE, EDGE), 0, 1),
        ((0, EDGE), EDGE + 2 * range_dev, -2),
    ]

    def halo_copy(u, j, forward=False):
        (first, count), to, by = halos[j]
        if forward:
            src = ext_ref.at[u, :, :, pl.ds(EDGE + first, count)]
        else:
            src = echo_ref.at[:, u, :, pl.ds(first, count)]
        return pltpu.make_async_remote_copy(
            src_ref=src,
            dst_ref=ext_ref.at[u, :, :, pl.ds(to, count)],
            send_sem=halo_send.at[u, j], recv_sem=halo_recv.at[u, j],
            device_id={"tile": lax.rem(t + by + tiles, tiles)}, device_id_type=MESH,
        )

    def sends(j):
        by = halos[j][2]
        return (t + by >= 0) & (t + by < tiles)

    def gets(j):
        by = halos[j][2]
        return (t - by >= 0) & (t - by < tiles)

    def halo_start(u, forward=False):
        for j in range(3):
            @pl.when(sends(j))
            def _():
                halo_copy(u, j, forward).start()

    def raw_copy(i):
        return pltpu.make_async_remote_copy(
            src_ref=echo_ref.at[:, RAW_FIRST + i],
            dst_ref=ext_ref.at[POLS + i, :, :, pl.ds(EDGE, range_dev)],
            send_sem=raw_send.at[i], recv_sem=raw_recv.at[i],
            device_id={"pulse": inner}, device_id_type=MESH,
        )

    def foot_copy():
        return pltpu.make_async_remote_copy(
            src_ref=foot_ref, dst_ref=far_foot, send_sem=foot_sem.at[0], recv_sem=foot_sem.at[1],
            device_id={"pulse": inner}, device_id_type=MESH,
        )

    halo_start(0)

    @pl.when(is_mid)
    def _():
        foot_copy().start()
        for i in range(RAW):
            raw_copy(i).start()

    for u in range(UNITS):
        for j in range(3):
            (_, count), to, _ = halos[j]

            @pl.when(jnp.logical_not(gets(j)))
            def _():
                ext_ref[u, :, :, to : to + count] = jnp.zeros((2, pulses, count), bf16)

    def order_blocks(feet):
        targets = []
        for f in range(blocks):
            rank = jnp.int32(0)
            for earlier in range(f):
                rank = rank + (feet[earlier] == feet[f]).astype(jnp.int32)
            targets.append(feet[f] * CAP + rank)
        sources = []
        for s in range(slots):
            source = jnp.int32(0)
            for f in range(blocks):
                source = source + f * (targets[f] == s).astype(jnp.int32)
            sources.append(source)
        return sources

    @pl.when(jnp.logical_not(is_mid))
    def _():
        for f in range(blocks):
            far_foot[0, f] = jnp.int32(0)

    sources = order_blocks([foot_ref[0, f] for f in range(blocks)])
    tab_row = iota((TABROWS, RBLOCK), 0)
    for f in range(blocks):
        index_f = index_ref[0, f : f + 1, :].astype(f32)
        frac_f = frac_ref[0, f : f + 1, :].astype(f32)
        landing = (slot_ref[0, f] + 1).astype(f32)
        table = jnp.where(tab_row == 0, index_f, jnp.where(tab_row == 1, frac_f, 0.0))
        wide_ref[f] = jnp.where(tab_row == 2, landing, table).astype(bf16)
    for s in range(slots):
        tab_ref[s] = wide_ref[sources[s]]

    def tab_copy(d, peer, place):
        return pltpu.make_async_remote_copy(
            src_ref=tab_ref.at[pl.ds(peer * CAP, CAP)],
            dst_ref=tabs.at[pl.ds(place * CAP, CAP)],
            send_sem=a2a_send.at[UNITS, d - 1], recv_sem=a2a_recv.at[UNITS, d - 1],
            device_id={"tile": peer}, device_id_type=MESH,
        )

    def unit_place(u):
        return jnp.where(u < POLS, g, inner), jnp.where(u < POLS, u, u - POLS + RAW_FIRST)

    def spread_copy(u, d, peer, place):
        group, pol = unit_place(u)
        return pltpu.make_async_remote_copy(
            src_ref=kid_ref.at[u, :, pl.ds(peer * CAP, CAP)],
            dst_ref=kids.at[group, pol, :, pl.ds(place * CAP, CAP)],
            send_sem=a2a_send.at[u, d - 1], recv_sem=a2a_recv.at[u, d - 1],
            device_id={"tile": peer}, device_id_type=MESH,
        )

    def spread_start(u):
        for d in range(1, tiles):
            spread_copy(u, d, lax.rem(t + d, tiles), t).start()
        group, pol = unit_place(u)
        kids[group, pol, :, pl.ds(t * CAP, CAP)] = kid_ref[u, :, pl.ds(t * CAP, CAP)]

    def spread_wait(u):
        for d in range(1, tiles):
            peer = lax.rem(t + tiles - d, tiles)
            spread_copy(u, d, peer, peer).wait_recv()

    def line_copy(k, group, lane, to):
        part = kids.at[group, k]
        return pltpu.make_async_remote_copy(
            src_ref=part, dst_ref=part,
            send_sem=line_send.at[lane, k], recv_sem=line_recv.at[group, k],
            device_id={"pulse": to}, device_id_type=MESH,
        )

    def line_tab(group, lane, to):
        part = packed_ref.at[group]
        return pltpu.make_async_remote_copy(
            src_ref=part, dst_ref=part,
            send_sem=line_send.at[lane, TAB], recv_sem=line_recv.at[group, TAB],
            device_id={"pulse": to}, device_id_type=MESH,
        )

    for d in range(1, tiles):
        tab_copy(d, lax.rem(t + d, tiles), t).start()
    tabs[pl.ds(t * CAP, CAP)] = tab_ref[pl.ds(t * CAP, CAP)]

    for part in range(2):
        line = replica_ref[part : part + 1, :].astype(f32)
        line = jnp.concatenate([line, jnp.zeros((1, CBLOCK), f32)], axis=1)
        rolled = pltpu.roll(
            jnp.broadcast_to(line, (CBLOCK, window)), 0, 1, stride=1, stride_axis=0
        )
        if part == 0:
            toep_ref[0:CBLOCK, 0:window] = rolled.astype(bf16)
            toep_ref[CBLOCK:, window:] = rolled.astype(bf16)
        else:
            toep_ref[0:CBLOCK, window:] = rolled.astype(bf16)
            toep_ref[CBLOCK:, 0:window] = (-rolled).astype(bf16)

    halo_start(jnp.where(is_mid, LAST, 1))

    row = iota((64, 16), 0)
    angle = jnp.zeros((64, 16), f32)
    for a in range(16):
        angle = jnp.where(((row >> 1) & 15) == a, steer_ref[a : a + 1, :], angle)
    on_row = iota((32, 32), 0) == iota((32, 32), 1)
    turns = [
        jnp.sum(jnp.where(on_row, phase_ref[c : c + 1, :], 0.0), axis=1, keepdims=True)
        for c in range(2)
    ]
    angle = angle + jnp.concatenate(turns, axis=0)
    scale = math.sqrt(0.5) / math.sqrt(steer_ref.shape[1])
    cosine, sine = jnp.cos(angle) * scale, jnp.sin(angle) * scale
    small = jnp.concatenate(
        [
            jnp.concatenate([cosine, -sine], axis=1),
            jnp.concatenate([sine, cosine], axis=1),
        ],
        axis=0,
    ).astype(bf16)
    o_at = iota((512, 128), 0)
    tall = ((o_at & 1) * 64 + (o_at >> 3) == iota((512, 128), 1)).astype(bf16)
    i_at = iota((32, 256), 1)
    broad = (((i_at >> 5) & 1) * 16 + (i_at & 15) == iota((32, 256), 0)).astype(bf16)
    spread = jnp.dot(tall, small, preferred_element_type=f32).astype(bf16)
    spread = jnp.dot(spread, broad, preferred_element_type=f32)
    o_all, i_all = iota((512, 256), 0), iota((512, 256), 1)
    same = (((o_all >> 1) & 3) == (i_all >> 6)) & ((o_all >> 8) == ((i_all >> 4) & 1))
    big_ref[...] = jnp.where(same, spread, 0.0).astype(bf16)
    o_all, i_all = iota((256, 256), 0), iota((256, 256), 1)
    order_in = (o_all & 31) * 8 + ((o_all >> 5) & 3) * 2 + (o_all >> 7)
    perm_ref[...] = (i_all == order_in).astype(bf16)

    @pl.when(is_mid)
    def _():
        foot_copy().wait_recv()

    far_sources = order_blocks([far_foot[0, f] for f in range(blocks)])

    def begin_tab():
        for d in range(1, tiles):
            peer = lax.rem(t + tiles - d, tiles)
            tab_copy(d, peer, peer).wait_recv()
        row, column = iota((3 * slots, slots * TABROWS), 0), iota((3 * slots, slots * TABROWS), 1)
        choose = column == (row & (slots - 1)) * TABROWS + row // slots
        packed_ref[g] = jnp.dot(
            choose.astype(bf16), tabs[...].reshape(slots * TABROWS, RBLOCK),
            preferred_element_type=f32,
        ).astype(bf16)
        line_tab(g, 0, inner).start()

    def relay(k):
        line_copy(k, end, 0, inner).wait_recv()
        line_copy(k, end, 1, inner).start()

    def form(u):
        @pl.when(u < POLS)
        def _():
            local_copy(u).wait()

        for j in range(3):
            @pl.when(gets(j))
            def _():
                halo_copy(u, j, True).wait_recv()

        @pl.when(u == 0)
        def _():
            halo_start(jnp.where(is_mid, 1, 2))

        pieces = []
        for j in range(9):
            start = j * CBLOCK
            pieces.append(
                jnp.concatenate(
                    [ext_ref[u, 0, :, start : start + window], ext_ref[u, 1, :, start : start + window]],
                    axis=1,
                )
            )
        found = lax.dot_general(
            jnp.concatenate(pieces, axis=0), toep_ref[...], (((1,), (1,)), ((), ())),
            preferred_element_type=f32,
        ).astype(bf16)
        before = (iota((pulses, 2 * CBLOCK), 1) & (CBLOCK - 1)) < EDGE
        first = jnp.where(before & (t == 0), 0.0, found[0:pulses].astype(f32)).astype(bf16)
        for jj in range(3):
            stacked = []
            for q in range(QUARTERS):
                at = 2 * q + jj
                one = first if at == 0 else found[at * pulses : (at + 1) * pulses]
                stacked += [one[:, :CBLOCK], one[:, CBLOCK:]]
            sub_ref[:, jj * CBLOCK : (jj + 1) * CBLOCK] = jnp.dot(
                big_ref[...], jnp.concatenate(stacked, axis=0), preferred_element_type=f32
            )

        def merge(b, carry):
            totals = [None] * 4
            for c in range(2):
                by = shift_ref[c, b]
                weight = blend_ref[c, b]
                back = by < 0
                turn = jnp.where(back, by + RBLOCK, by)
                x = sub_ref[pl.ds(pl.multiple_of((c * 32 + b) * 8, 8), 8), :]
                x = jnp.concatenate([x[:, i * RBLOCK : (i + 1) * RBLOCK] for i in range(6)], axis=0)
                x = jnp.where(back, x[:40], x[8:])
                low = pltpu.roll(x, (RBLOCK - turn) & (RBLOCK - 1), 1)
                high = pltpu.roll(x, RBLOCK - 1 - turn, 1)
                lane = iota((32, RBLOCK), 1)
                low = jnp.where(lane < RBLOCK - turn, low[:32], low[8:])
                high = jnp.where(lane < RBLOCK - 1 - turn, high[:32], high[8:])
                y = (1.0 - weight) * low + weight * high
                totals = y if c == 0 else totals + y
            for i in range(4):
                merged_ref[pl.ds(pl.multiple_of(b * 8, 8), 8), i * RBLOCK : (i + 1) * RBLOCK] = (
                    totals[i * 8 : (i + 1) * 8]
                )
            return carry

        lax.fori_loop(0, 32, merge, 0, unroll=UNROLL)
        ordered = jnp.dot(
            perm_ref[...], merged_ref[...].astype(bf16), preferred_element_type=f32
        ).astype(bf16)
        for part in range(2):
            for f in range(blocks):
                at = (part * QUARTERS + f // 4) * 32
                block_ref[f, part] = ordered[at : at + 32, (f % 4) * RBLOCK : (f % 4 + 1) * RBLOCK]
        for s in range(slots):
            kid_ref[u, :, s] = block_ref[jnp.where(u < POLS, sources[s], far_sources[s])]
        spread_start(u)

    def own_line(k):
        spread_wait(k)
        line_copy(k, g, 0, inner).start()

    def forward(i):
        raw_copy(i).wait_recv()
        halo_start(POLS + i, True)

    middle = spans // 2 * RBLOCK

    def part_copy(k, half, to, place):
        span = pl.ds(half * middle, middle)
        return pltpu.make_async_remote_copy(
            src_ref=part_ref.at[k, :, :, span], dst_ref=arrived_ref.at[place, :, :, span],
            send_sem=part_send.at[k, half], recv_sem=part_recv.at[place, half],
            device_id={"pulse": to}, device_id_type=MESH,
        )

    def prepare(ref, group, beam_group, row, column, used):
        expand = (
            (iota((RBLOCK, lanes), 1) & (beams - 1)) + beam_group * beams
            == iota((RBLOCK, lanes), 0)
        ).astype(bf16)
        where_at = (iota((1, lanes), 1) // beams + 1).astype(f32)
        child = iota((32, lanes), 0).astype(f32)

        wide = jnp.dot(packed_ref[group], expand, preferred_element_type=f32)
        for at in range(slots // 4):
            pieces = []
            for slot in range(at * 4, at * 4 + 4):
                landing = wide[2 * slots + slot : 2 * slots + slot + 1, :]
                index = jnp.where(
                    (landing == where_at) & used, wide[slot : slot + 1, :], -9.0
                )
                frac = wide[slots + slot : slots + slot + 1, :]
                lower = (1.0 - frac).astype(bf16).astype(f32)
                weight = jnp.where(child == index, lower, 0.0)
                pieces.append(jnp.where(child == index + 1.0, frac, weight))
            block = jnp.concatenate(pieces, axis=0)
            at_column = pl.multiple_of(column + at * 128, 128)
            ref[row : row + lanes, pl.ds(at_column, 128)] = block.T.astype(bf16)

    def put(ref, k, half, result):
        for step in range(spans // 2):
            w = half * (spans // 2) + step
            for i in range(2):
                ref[k, i, :, w * RBLOCK : (w + 1) * RBLOCK] = result[
                    step * beams : (step + 1) * beams, i * RBLOCK : (i + 1) * RBLOCK
                ]

    side = jnp.where(g < 2, 0, 2)

    def prepare_all():
        line_tab(inner, 0, inner).wait_recv()
        line_tab(far, 0, inner).wait_recv()

        def prepare_group(group, carry):
            column = pl.multiple_of(group * depth, 128)
            prepare(left_ref, group, g, 0, column, group >= 0)

            @pl.when(group != g)
            def _():
                prepare(left_ref, group, end, lanes, column, group != end)

            return carry

        lax.fori_loop(0, 4, prepare_group, 0)

        def prepare_cross(at, carry):
            column = pl.multiple_of(at * depth, 128)
            prepare(cross_ref, side + at, far, 0, column, at >= 0)
            prepare(cross_ref, side + at, inner, lanes, column, at >= 0)
            return carry

        lax.fori_loop(0, 2, prepare_cross, 0)

    def final(k):
        line_copy(k, far, 0, inner).wait_recv()
        right = jnp.concatenate(
            [kids[:, k, i].reshape(4 * depth, RBLOCK) for i in range(2)], axis=1
        )
        for half in range(2):
            first = lanes + half * (lanes // 2)
            put(part_ref, k, half, jnp.dot(
                left_ref[first : first + lanes // 2, :], right, preferred_element_type=f32
            ).astype(bf16))
            part_copy(k, half, end, k).start()
        for half in range(2):
            first = half * (lanes // 2)
            result = jnp.dot(
                left_ref[first : first + lanes // 2, :], right, preferred_element_type=f32
            ).astype(bf16)
            for step in range(spans // 2):
                w = half * (spans // 2) + step
                for i in range(2):
                    out_ref[i, k, :, w * RBLOCK : (w + 1) * RBLOCK] = result[
                        step * beams : (step + 1) * beams, i * RBLOCK : (i + 1) * RBLOCK
                    ]

    def cross():
        line_copy(LAST, end, 0, inner).wait_recv()
        right = jnp.concatenate(
            [kids[pl.ds(side, 2), LAST, i].reshape(2 * depth, RBLOCK) for i in range(2)], axis=1
        )
        for at in range(2):
            for half in range(2):
                first = at * lanes + half * (lanes // 2)
                put(part_ref, POLS + at, half, jnp.dot(
                    cross_ref[first : first + lanes // 2, :], right, preferred_element_type=f32
                ).astype(bf16))
                part_copy(POLS + at, half, inner if at else far, POLS).start()
        columns = pl.ds(pl.multiple_of(side * depth, 128), 2 * depth)
        for half in range(2):
            first = half * (lanes // 2)
            put(own_ref, LAST, half, jnp.dot(
                left_ref[first : first + lanes // 2, columns], right, preferred_element_type=f32
            ))

    def last_part():
        right = jnp.concatenate(
            [kids[g, LAST, i].reshape(depth, RBLOCK) for i in range(2)], axis=1
        )
        columns = pl.ds(pl.multiple_of(g * depth, 128), depth)
        for half in range(2):
            first = lanes + half * (lanes // 2)
            put(part_ref, LAST, half, jnp.dot(
                left_ref[first : first + lanes // 2, columns], right, preferred_element_type=f32
            ).astype(bf16))
            part_copy(LAST, half, end, LAST).start()

    def mid_unit(u):
        return u // 2 + 3 * (u % 2)

    def step(i, carry):
        @pl.when(is_mid & (i == 3))
        def _():
            prepare(left_ref, g, end, lanes, pl.multiple_of(g * depth, 128), g >= 0)
            spread_wait(LAST)
            last_part()
            relay(0)

        @pl.when(is_mid & (i == 4))
        def _():
            prepare_all()
            relay(1)
            line_copy(0, inner, 0, inner).wait_recv()
            final(0)

        form(jnp.where(is_mid, mid_unit(i), i))

        @pl.when(i == 0)
        def _():
            begin_tab()

        @pl.when(jnp.logical_not(is_mid) & (i >= 1))
        def _():
            own_line(i - 1)

        @pl.when(is_mid & (i == 1))
        def _():
            own_line(0)
            forward(0)

        @pl.when(i == 1)
        def _():
            halo_start(jnp.where(is_mid, 2, 3))

        @pl.when(is_mid & (i == 2))
        def _():
            line_tab(end, 0, inner).wait_recv()
            line_tab(end, 1, inner).start()
            forward(1)

        @pl.when(is_mid & (i == 4))
        def _():
            relay(2)

        return carry

    units = jnp.where(is_mid, UNITS, POLS)
    lax.fori_loop(0, units, step, 0)

    @pl.when(is_mid)
    def _():
        spread_wait(1)
        spread_wait(POLS)

        def later(k, carry):
            final(k)

            @pl.when(k == 1)
            def _():
                cross()
                spread_wait(2)
                spread_wait(POLS + 1)

            return carry

        lax.fori_loop(1, LAST, later, 0)
        for half in range(2):
            part_copy(POLS + 1, half, inner, POLS).wait_recv()
            span = slice(half * middle, (half + 1) * middle)
            for i in range(2):
                out_ref[i, LAST, :, span] = (
                    own_ref[LAST, i, :, span] + arrived_ref[POLS, i, :, span].astype(f32)
                ).astype(bf16)
        line_tab(g, 0, inner).wait_send()
        line_tab(end, 1, inner).wait_send()
        line_copy(0, g, 0, inner).wait_send()
        for k in range(LAST):
            line_copy(k, end, 1, inner).wait_send()
        for half in range(2):
            for k in range(POLS):
                part_copy(k, half, end, k).wait_send()
            part_copy(POLS, half, far, POLS).wait_send()
            part_copy(POLS + 1, half, inner, POLS).wait_send()
        foot_copy().wait_send()
        for i in range(RAW):
            raw_copy(i).wait_send()

    @pl.when(jnp.logical_not(is_mid))
    def _():
        own_line(LAST)
        prepare(left_ref, g, g, 0, 0, g >= 0)

        def product(k, carry):
            right = jnp.concatenate(
                [kids[g, k, i].reshape(depth, RBLOCK) for i in range(2)], axis=1
            )
            for half in range(2):
                first = half * (lanes // 2)
                put(own_ref, k, half, jnp.dot(
                    left_ref[first : first + lanes // 2, :depth], right,
                    preferred_element_type=f32,
                ))
            return carry

        lax.fori_loop(0, POLS, product, 0)

        def finish(k, carry):
            for half in range(2):
                part_copy(k, half, inner, k).wait_recv()
                span = slice(half * middle, (half + 1) * middle)
                for i in range(2):
                    out_ref[i, k, :, span] = (
                        own_ref[k, i, :, span] + arrived_ref[k, i, :, span].astype(f32)
                    ).astype(bf16)
            return carry

        lax.fori_loop(0, LAST, finish, 0)
        for half in range(2):
            part_copy(LAST, half, inner, LAST).wait_recv()
            part_copy(POLS, half, inner, POLS).wait_recv()
            span = slice(half * middle, (half + 1) * middle)
            for i in range(2):
                out_ref[i, LAST, :, span] = (
                    own_ref[LAST, i, :, span]
                    + arrived_ref[LAST, i, :, span].astype(f32)
                    + arrived_ref[POLS, i, :, span].astype(f32)
                ).astype(bf16)
        line_tab(g, 0, inner).wait_send()
        for k in range(POLS):
            line_copy(k, g, 0, inner).wait_send()

    for d in range(1, tiles):
        tab_copy(d, lax.rem(t + d, tiles), t).wait_send()

    def drain(u, carry):
        for d in range(1, tiles):
            spread_copy(u, d, lax.rem(t + d, tiles), t).wait_send()
        for j in range(3):
            @pl.when(sends(j))
            def _():
                halo_copy(u, j, True).wait_send()
        return carry

    lax.fori_loop(0, units, drain, 0)


def fused(
    shift, blend, foot, slot, echoes, replica, steer_phase, merge_phase, index, frac,
    tiles, beams, range_dev,
):
    slots = tiles * CAP
    lanes = range_dev // RBLOCK * beams
    bf16 = jnp.bfloat16
    f32 = jnp.float32
    pulses = echoes.shape[2]
    vmem = pl.BlockSpec(memory_space=pltpu.VMEM)
    smem = pl.BlockSpec(memory_space=pltpu.SMEM)
    dma = pltpu.SemaphoreType.DMA
    return pl.pallas_call(
        functools.partial(fused_kernel, tiles),
        out_shape=jax.ShapeDtypeStruct((2, POLS, beams, range_dev), bf16),
        in_specs=[smem] * 4 + [pl.BlockSpec(memory_space=pl.ANY)] + [vmem] * 5,
        out_specs=vmem,
        scratch_shapes=[
            pltpu.VMEM((UNITS, 2, pulses, 2 * range_dev + 2 * EDGE), bf16),
            pltpu.VMEM((2 * CBLOCK, 2 * (CBLOCK + replica.shape[1])), bf16),
            pltpu.VMEM((512, 256), bf16),
            pltpu.VMEM((256, 256), bf16),
            pltpu.VMEM((512, 3 * CBLOCK), f32),
            pltpu.VMEM((256, 4 * RBLOCK), f32),
            pltpu.VMEM((slots, 2, 32, RBLOCK), bf16),
            pltpu.VMEM((UNITS, 2, slots, 32, RBLOCK), bf16),
            pltpu.VMEM((slots, TABROWS, RBLOCK), bf16),
            pltpu.VMEM((slots, TABROWS, RBLOCK), bf16),
            pltpu.VMEM((4, POLS, 2, slots, 32, RBLOCK), bf16),
            pltpu.VMEM((slots, TABROWS, RBLOCK), bf16),
            pltpu.VMEM((4, 3 * slots, RBLOCK), bf16),
            pltpu.VMEM((2 * lanes, 4 * slots * 32), bf16),
            pltpu.VMEM((2 * lanes, 2 * slots * 32), bf16),
            pltpu.VMEM((POLS + 2, 2, beams, range_dev), bf16),
            pltpu.VMEM((POLS + 1, 2, beams, range_dev), bf16),
            pltpu.VMEM((POLS, 2, beams, range_dev), f32),
            pltpu.SMEM((1, range_dev // RBLOCK), jnp.int32),
            dma((POLS,)),
            dma((2,)),
            dma((RAW,)),
            dma((RAW,)),
            dma((UNITS, 3)),
            dma((UNITS, 3)),
            dma((UNITS + 1, tiles - 1)),
            dma((UNITS + 1, tiles - 1)),
            dma((2, POLS + 1)),
            dma((4, POLS + 1)),
            dma((POLS + 2, 2)),
            dma((POLS + 1, 2)),
        ],
        compiler_params=pltpu.CompilerParams(
            collective_id=0, has_side_effects=True, vmem_limit_bytes=40 << 20
        ),
    )(shift, blend, foot, slot, echoes, replica, steer_phase, merge_phase, index, frac)


def shards(
    echoes, replica, steer_phase, range_shift, merge_phase, merge_frac,
    footprint, row_slot, beam_index, beam_frac,
):
    pulse_count, pol_count, range_dev = echoes.shape[1:]
    rows = pulse_count * pol_count
    taps = replica.shape[1]
    final_beams = beam_index.shape[2]
    tiles = lax.axis_size("tile")
    groups = lax.axis_size("pulse")
    slot_count = tiles * CAP
    scale = 1.0 / math.sqrt(steer_phase.shape[1])
    steer_re = jnp.cos(steer_phase) * scale
    steer_im = jnp.sin(steer_phase) * scale
    steer = jnp.concatenate(
        [
            jnp.concatenate([steer_re, -steer_im], axis=1),
            jnp.concatenate([steer_im, steer_re], axis=1),
        ],
        axis=0,
    ).astype(jnp.bfloat16)
    half_root = math.sqrt(0.5)
    coef = jnp.stack(
        [
            merge_frac.reshape(-1),
            (jnp.cos(merge_phase) * half_root).reshape(-1),
            (jnp.sin(merge_phase) * half_root).reshape(-1),
        ]
    )
    beams = final_beams // groups
    if groups == 4 and slot_count == range_dev // RBLOCK:
        return fused(
            range_shift, merge_frac, footprint, row_slot, echoes.transpose(0, 2, 1, 3),
            replica, steer_phase, merge_phase, beam_index, beam_frac, tiles, beams, range_dev,
        )
    own = echoes.reshape(2, rows, range_dev)
    following = shifted(own, "tile", -1)
    before = shifted(own[:, :, range_dev - EDGE :], "tile", 1)
    after = shifted(own[:, :, :EDGE], "tile", -2)

    width = range_dev + CBLOCK
    smem = pl.BlockSpec(memory_space=pltpu.SMEM)
    vmem = pl.BlockSpec(memory_space=pltpu.VMEM)
    kids, tabs = pl.pallas_call(
        form_kernel,
        out_shape=(
            jax.ShapeDtypeStruct((8, slot_count, 32, RBLOCK), jnp.bfloat16),
            jax.ShapeDtypeStruct((slot_count, TABROWS, RBLOCK), jnp.bfloat16),
        ),
        in_specs=[smem] * 4 + [vmem] * 8,
        out_specs=(vmem, vmem),
        scratch_shapes=[
            pltpu.VMEM((2, rows, 2 * range_dev + 2 * EDGE), jnp.bfloat16),
            pltpu.VMEM((2 * CBLOCK, 2 * (CBLOCK + taps)), jnp.bfloat16),
            pltpu.VMEM((256, width), jnp.float32),
            pltpu.VMEM((256, range_dev), jnp.bfloat16),
        ],
        compiler_params=pltpu.CompilerParams(vmem_limit_bytes=56 << 20),
    )(
        range_shift, coef, footprint, row_slot,
        own, following, before, after, replica, steer, beam_index, beam_frac,
    )
    sent = jnp.concatenate(
        [kids.transpose(1, 0, 2, 3).reshape(slot_count, 256, RBLOCK), tabs], axis=1
    )
    got = lax.all_to_all(
        sent.reshape(tiles, CAP, 256 + TABROWS, RBLOCK), "tile",
        split_axis=0, concat_axis=0, tiled=True,
    ).reshape(slot_count, 256 + TABROWS, RBLOCK)
    gathered = lax.all_gather(got, "pulse", axis=0, tiled=True)
    total_slots = groups * slot_count
    image = pl.pallas_call(
        place_kernel,
        out_shape=jax.ShapeDtypeStruct((2 * pol_count, beams, range_dev), jnp.bfloat16),
        in_specs=[vmem],
        out_specs=vmem,
        scratch_shapes=[
            pltpu.VMEM((total_slots * 32, range_dev // RBLOCK * beams), jnp.bfloat16),
            pltpu.VMEM((total_slots * 32, 8 * RBLOCK), jnp.bfloat16),
        ],
        compiler_params=pltpu.CompilerParams(vmem_limit_bytes=56 << 20),
    )(gathered)
    return image.reshape(2, pol_count, beams, range_dev)


def solution(mesh):
    placed = (
        P(None, "pulse", None, "tile"),
        P(),
        P(),
        P(),
        P(),
        P(),
        P("pulse", "tile"),
        P("pulse", "tile"),
        P("pulse", "tile", None),
        P("pulse", "tile", None),
    )
    return jax.shard_map(
        shards,
        mesh=mesh,
        in_specs=placed,
        out_specs=P(None, None, "pulse", "tile"),
        check_vma=False,
    )
```

```python
import functools
import math

import jax
import jax.numpy as jnp
from jax import lax
from jax.experimental import pallas as pl
from jax.experimental.pallas import tpu as pltpu
from jax.sharding import PartitionSpec as P

RBLOCK = 128
CAP = 2
CBLOCK = 256
EDGE = 128
TABROWS = 16


def shifted(value, axis, by):
    count = lax.axis_size(axis)
    pairs = [(i, i + by) for i in range(count) if 0 <= i + by < count]
    return lax.ppermute(value, axis, pairs)


def iota(shape, dim):
    return lax.broadcasted_iota(jnp.int32, shape, dim)


def form_kernel(
    shift_ref, coef_ref, foot_ref, slot_ref,
    own_ref, next_ref, prev_ref, after_ref, replica_ref, steer_ref, index_ref, frac_ref,
    kid_ref, tab_ref,
    ext_ref, toep_ref, sub_ref, merged_ref,
):
    range_dev = own_ref.shape[2]
    rows = own_ref.shape[1]
    taps = replica_ref.shape[1]
    window = CBLOCK + taps
    width = sub_ref.shape[1]
    blocks = range_dev // RBLOCK
    bf16 = jnp.bfloat16

    ext_ref[:, :, 0:EDGE] = prev_ref[...]
    ext_ref[:, :, EDGE : EDGE + range_dev] = own_ref[...]
    ext_ref[:, :, EDGE + range_dev : EDGE + 2 * range_dev] = next_ref[...]
    ext_ref[:, :, EDGE + 2 * range_dev :] = after_ref[...]

    for part in range(2):
        line = replica_ref[part : part + 1, :].astype(jnp.float32)
        line = jnp.concatenate([line, jnp.zeros((1, CBLOCK), jnp.float32)], axis=1)
        rolled = pltpu.roll(
            jnp.broadcast_to(line, (CBLOCK, window)), 0, 1, stride=1, stride_axis=0
        )
        if part == 0:
            toep_ref[0:CBLOCK, 0:window] = rolled.astype(bf16)
            toep_ref[CBLOCK:, window:] = rolled.astype(bf16)
        else:
            toep_ref[0:CBLOCK, window:] = rolled.astype(bf16)
            toep_ref[CBLOCK:, 0:window] = (-rolled).astype(bf16)

    r_at = iota((256, 32), 0)
    left = (((r_at >> 2) & 1) * 16 + ((r_at >> 3) & 15) == iota((256, 32), 1)).astype(bf16)
    k_at = iota((32, 256), 1)
    right = ((k_at >> 7) * 16 + ((k_at >> 2) & 15) == iota((32, 256), 0)).astype(bf16)
    spread = jnp.dot(left, steer_ref[...], preferred_element_type=jnp.float32).astype(bf16)
    spread = jnp.dot(spread, right, preferred_element_type=jnp.float32)
    r_all, k_all = iota((256, 256), 0), iota((256, 256), 1)
    same = ((r_all >> 7) == ((k_all >> 6) & 1)) & ((r_all & 3) == (k_all & 3))
    steer = jnp.where(same, spread, 0.0).astype(bf16)

    group = 3

    def compress(at, carry):
        pieces = []
        for step in range(group):
            start = pl.multiple_of((at * group + step) * CBLOCK, CBLOCK)
            pieces.append(
                jnp.concatenate(
                    [ext_ref[0, :, pl.ds(start, window)], ext_ref[1, :, pl.ds(start, window)]],
                    axis=1,
                )
            )
        left_side = jnp.concatenate(pieces, axis=0)
        found = lax.dot_general(
            left_side, toep_ref[...], (((1,), (1,)), ((), ())),
            preferred_element_type=jnp.float32,
        ).astype(bf16)
        for step in range(group):
            start = pl.multiple_of((at * group + step) * CBLOCK, CBLOCK)
            one = found[step * rows : (step + 1) * rows]
            stacked = jnp.concatenate([one[:, :CBLOCK], one[:, CBLOCK:]], axis=0)
            sub = jnp.dot(steer, stacked, preferred_element_type=jnp.float32)
            sub_ref[:, pl.ds(start, CBLOCK)] = sub.astype(bf16).astype(jnp.float32)
        return carry

    lax.fori_loop(0, width // (CBLOCK * group), compress, 0)

    @pl.when(lax.axis_index("tile") == 0)
    def _():
        sub_ref[:, 0:EDGE] = jnp.zeros((256, EDGE), jnp.float32)

    sign = jnp.where(iota((8, width), 0) < 4, -1.0, 1.0).astype(jnp.float32)

    def merge(a, carry):
        totals = [None, None]
        for c in range(2):
            x = sub_ref[pl.ds(pl.multiple_of((c * 16 + a) * 8, 8), 8), :]
            x_up = pltpu.roll(x, width - 1, 1)
            for parity in range(2):
                b = 2 * a + parity
                weight = coef_ref[0, c * 32 + b]
                cosine = coef_ref[1, c * 32 + b]
                sine = coef_ref[2, c * 32 + b]
                y = (1.0 - weight) * x + weight * x_up
                v = cosine * y + (sine * sign) * pltpu.roll(y, 4, 0)
                by = shift_ref[c, b]
                z = pltpu.roll(v, jnp.where(by > 0, width - by, -by), 1)
                z = z[:, EDGE : EDGE + range_dev]
                totals[parity] = z if totals[parity] is None else totals[parity] + z
        merged_ref[pl.ds(pl.multiple_of(a * 16, 16), 16), :] = jnp.concatenate(
            totals, axis=0
        ).astype(bf16)
        return carry

    lax.fori_loop(0, 16, merge, 0)

    order = (k_all == (r_all & 31) * 8 + (r_all >> 5)).astype(bf16)
    if tab_ref.shape[0] > blocks:
        kid_ref[...] = jnp.zeros(kid_ref.shape, bf16)
        tab_ref[...] = jnp.zeros(tab_ref.shape, bf16)
    tab_row = iota((TABROWS, RBLOCK), 0)
    for f in range(blocks):
        foot = foot_ref[0, f]
        rank = jnp.int32(0)
        for before in range(f):
            rank = rank + (foot_ref[0, before] == foot).astype(jnp.int32)
        slot = foot * CAP + rank
        part = jnp.dot(
            order, merged_ref[:, f * RBLOCK : (f + 1) * RBLOCK],
            preferred_element_type=jnp.float32,
        )
        kid_ref[:, slot] = part.astype(bf16).reshape(8, 32, RBLOCK)
        landing = (slot_ref[0, f] + 1).astype(jnp.float32)
        index_f = index_ref[0, f : f + 1, :].astype(jnp.float32)
        frac_f = frac_ref[0, f : f + 1, :].astype(jnp.float32)
        table = jnp.where(tab_row == 0, index_f, jnp.where(tab_row == 1, frac_f, 0.0))
        table = jnp.where(tab_row == 2, landing, table)
        tab_ref[slot] = table.astype(bf16)


def place_kernel(got_ref, out_ref, left_ref, right_ref):
    slots = got_ref.shape[0]
    beams = out_ref.shape[1]
    spans = out_ref.shape[2] // RBLOCK
    lanes = spans * beams
    mine = lax.axis_index("pulse") * beams
    bf16 = jnp.bfloat16
    lane = iota((RBLOCK, lanes), 1)
    widen = ((lane & (beams - 1)) + mine == iota((RBLOCK, lanes), 0)).astype(bf16)
    where_at = iota((1, lanes), 1) // beams + 1
    child = iota((32, lanes), 0).astype(jnp.float32)

    def prepare(at, carry):
        table = got_ref[at, 256 : 256 + TABROWS, :]
        wide = jnp.dot(table, widen, preferred_element_type=jnp.float32)
        landing = wide[2:3, :]
        index = jnp.where(landing == where_at.astype(jnp.float32), wide[0:1, :], -9.0)
        frac = wide[1:2, :]
        lower = (1.0 - frac).astype(bf16).astype(jnp.float32)
        weight = jnp.where(child == index, lower, 0.0)
        weight = jnp.where(child == index + 1.0, frac, weight)
        start = pl.multiple_of(at * 32, 32)
        left_ref[pl.ds(start, 32), :] = weight.astype(bf16)
        for x in range(8):
            right_ref[pl.ds(start, 32), x * RBLOCK : (x + 1) * RBLOCK] = got_ref[
                at, x * 32 : (x + 1) * 32, :
            ]
        return carry

    lax.fori_loop(0, slots, prepare, 0)
    for half in range(0, lanes, 256):
        result = lax.dot_general(
            left_ref[:, half : half + 256], right_ref[...], (((0,), (0,)), ((), ())),
            preferred_element_type=jnp.float32,
        ).astype(bf16)
        for sub in range(256 // beams):
            w = half // beams + sub
            for x in range(8):
                out_ref[x, :, w * RBLOCK : (w + 1) * RBLOCK] = result[
                    sub * beams : (sub + 1) * beams, x * RBLOCK : (x + 1) * RBLOCK
                ]


MESH = pl.DeviceIdType.MESH
POLS = 4
RAW = 2
UNITS = POLS + RAW
RAW_FIRST = 1
LAST = POLS - 1
TAB = POLS
QUARTERS = 4
UNROLL = 16


def fused_kernel(
    tiles, shift_ref, blend_ref, foot_ref, slot_ref,
    echo_ref, replica_ref, steer_ref, phase_ref, index_ref, frac_ref, out_ref,
    ext_ref, toep_ref, big_ref, perm_ref, sub_ref, merged_ref, block_ref, kid_ref, tab_ref, wide_ref,
    kids, tabs, packed_ref, left_ref, cross_ref, part_ref, arrived_ref, own_ref,
    far_foot,
    local_sem, foot_sem, raw_send, raw_recv, halo_send, halo_recv,
    a2a_send, a2a_recv, line_send, line_recv, part_send, part_recv,
):
    g = lax.axis_index("pulse")
    t = lax.axis_index("tile")
    beams = out_ref.shape[2]
    range_dev = out_ref.shape[3]
    spans = range_dev // RBLOCK
    lanes = spans * beams
    slots = tiles * CAP
    depth = slots * 32
    pulses = echo_ref.shape[2]
    taps = replica_ref.shape[1]
    window = CBLOCK + taps
    blocks = spans

    bf16 = jnp.bfloat16
    f32 = jnp.float32
    is_mid = (g == 1) | (g == 2)
    inner = jnp.where(g == 0, 1, jnp.where(g == 1, 2, jnp.where(g == 2, 1, 2)))
    end = jnp.where(g < 2, 0, 3)
    far = 3 - end

    barrier = pltpu.get_barrier_semaphore()
    for d in range(1, tiles):
        pl.semaphore_signal(
            barrier, inc=1, device_id={"tile": lax.rem(t + d, tiles)}, device_id_type=MESH
        )
    pl.semaphore_signal(barrier, inc=1, device_id={"pulse": inner}, device_id_type=MESH)

    @pl.when(is_mid)
    def _():
        pl.semaphore_signal(barrier, inc=1, device_id={"pulse": end}, device_id_type=MESH)

    @pl.when(jnp.logical_not(is_mid))
    def _():
        pl.semaphore_signal(barrier, inc=1, device_id={"pulse": 3 - inner}, device_id_type=MESH)

    def local_copy(u):
        return pltpu.make_async_copy(
            echo_ref.at[:, u], ext_ref.at[u, :, :, pl.ds(EDGE, range_dev)], local_sem.at[u]
        )

    for u in range(POLS):
        local_copy(u).start()

    @pl.when(is_mid)
    def _():
        pl.semaphore_wait(barrier, tiles + 2)

    @pl.when(jnp.logical_not(is_mid))
    def _():
        pl.semaphore_wait(barrier, tiles)

    halos = [
        ((0, range_dev), EDGE + range_dev, -1),
        ((range_dev - EDGE, EDGE), 0, 1),
        ((0, EDGE), EDGE + 2 * range_dev, -2),
    ]

    def halo_copy(u, j, forward=False):
        (first, count), to, by = halos[j]
        if forward:
            src = ext_ref.at[u, :, :, pl.ds(EDGE + first, count)]
        else:
            src = echo_ref.at[:, u, :, pl.ds(first, count)]
        return pltpu.make_async_remote_copy(
            src_ref=src,
            dst_ref=ext_ref.at[u, :, :, pl.ds(to, count)],
            send_sem=halo_send.at[u, j], recv_sem=halo_recv.at[u, j],
            device_id={"tile": lax.rem(t + by + tiles, tiles)}, device_id_type=MESH,
        )

    def sends(j):
        by = halos[j][2]
        return (t + by >= 0) & (t + by < tiles)

    def gets(j):
        by = halos[j][2]
        return (t - by >= 0) & (t - by < tiles)

    def halo_start(u, forward=False):
        for j in range(3):
            @pl.when(sends(j))
            def _():
                halo_copy(u, j, forward).start()

    def raw_copy(i):
        return pltpu.make_async_remote_copy(
            src_ref=echo_ref.at[:, RAW_FIRST + i],
            dst_ref=ext_ref.at[POLS + i, :, :, pl.ds(EDGE, range_dev)],
            send_sem=raw_send.at[i], recv_sem=raw_recv.at[i],
            device_id={"pulse": inner}, device_id_type=MESH,
        )

    def foot_copy():
        return pltpu.make_async_remote_copy(
            src_ref=foot_ref, dst_ref=far_foot, send_sem=foot_sem.at[0], recv_sem=foot_sem.at[1],
            device_id={"pulse": inner}, device_id_type=MESH,
        )

    halo_start(0)

    @pl.when(is_mid)
    def _():
        foot_copy().start()
        for i in range(RAW):
            raw_copy(i).start()

    for u in range(UNITS):
        for j in range(3):
            (_, count), to, _ = halos[j]

            @pl.when(jnp.logical_not(gets(j)))
            def _():
                ext_ref[u, :, :, to : to + count] = jnp.zeros((2, pulses, count), bf16)

    def order_blocks(feet):
        targets = []
        for f in range(blocks):
            rank = jnp.int32(0)
            for earlier in range(f):
                rank = rank + (feet[earlier] == feet[f]).astype(jnp.int32)
            targets.append(feet[f] * CAP + rank)
        sources = []
        for s in range(slots):
            source = jnp.int32(0)
            for f in range(blocks):
                source = source + f * (targets[f] == s).astype(jnp.int32)
            sources.append(source)
        return sources

    @pl.when(jnp.logical_not(is_mid))
    def _():
        for f in range(blocks):
            far_foot[0, f] = jnp.int32(0)

    sources = order_blocks([foot_ref[0, f] for f in range(blocks)])
    tab_row = iota((TABROWS, RBLOCK), 0)
    for f in range(blocks):
        index_f = index_ref[0, f : f + 1, :].astype(f32)
        frac_f = frac_ref[0, f : f + 1, :].astype(f32)
        landing = (slot_ref[0, f] + 1).astype(f32)
        table = jnp.where(tab_row == 0, index_f, jnp.where(tab_row == 1, frac_f, 0.0))
        wide_ref[f] = jnp.where(tab_row == 2, landing, table).astype(bf16)
    for s in range(slots):
        tab_ref[s] = wide_ref[sources[s]]

    def tab_copy(d, peer, place):
        return pltpu.make_async_remote_copy(
            src_ref=tab_ref.at[pl.ds(peer * CAP, CAP)],
            dst_ref=tabs.at[pl.ds(place * CAP, CAP)],
            send_sem=a2a_send.at[UNITS, d - 1], recv_sem=a2a_recv.at[UNITS, d - 1],
            device_id={"tile": peer}, device_id_type=MESH,
        )

    def unit_place(u):
        return jnp.where(u < POLS, g, inner), jnp.where(u < POLS, u, u - POLS + RAW_FIRST)

    def spread_copy(u, d, peer, place):
        group, pol = unit_place(u)
        return pltpu.make_async_remote_copy(
            src_ref=kid_ref.at[u, :, pl.ds(peer * CAP, CAP)],
            dst_ref=kids.at[group, pol, :, pl.ds(place * CAP, CAP)],
            send_sem=a2a_send.at[u, d - 1], recv_sem=a2a_recv.at[u, d - 1],
            device_id={"tile": peer}, device_id_type=MESH,
        )

    def spread_start(u):
        for d in range(1, tiles):
            spread_copy(u, d, lax.rem(t + d, tiles), t).start()
        group, pol = unit_place(u)
        kids[group, pol, :, pl.ds(t * CAP, CAP)] = kid_ref[u, :, pl.ds(t * CAP, CAP)]

    def spread_wait(u):
        for d in range(1, tiles):
            peer = lax.rem(t + tiles - d, tiles)
            spread_copy(u, d, peer, peer).wait_recv()

    def line_copy(k, group, lane, to):
        part = kids.at[group, k]
        return pltpu.make_async_remote_copy(
            src_ref=part, dst_ref=part,
            send_sem=line_send.at[lane, k], recv_sem=line_recv.at[group, k],
            device_id={"pulse": to}, device_id_type=MESH,
        )

    def line_tab(group, lane, to):
        part = packed_ref.at[group]
        return pltpu.make_async_remote_copy(
            src_ref=part, dst_ref=part,
            send_sem=line_send.at[lane, TAB], recv_sem=line_recv.at[group, TAB],
            device_id={"pulse": to}, device_id_type=MESH,
        )

    for d in range(1, tiles):
        tab_copy(d, lax.rem(t + d, tiles), t).start()
    tabs[pl.ds(t * CAP, CAP)] = tab_ref[pl.ds(t * CAP, CAP)]

    for part in range(2):
        line = replica_ref[part : part + 1, :].astype(f32)
        line = jnp.concatenate([line, jnp.zeros((1, CBLOCK), f32)], axis=1)
        rolled = pltpu.roll(
            jnp.broadcast_to(line, (CBLOCK, window)), 0, 1, stride=1, stride_axis=0
        )
        if part == 0:
            toep_ref[0:CBLOCK, 0:window] = rolled.astype(bf16)
            toep_ref[CBLOCK:, window:] = rolled.astype(bf16)
        else:
            toep_ref[0:CBLOCK, window:] = rolled.astype(bf16)
            toep_ref[CBLOCK:, 0:window] = (-rolled).astype(bf16)

    halo_start(LAST)

    row = iota((64, 16), 0)
    angle = jnp.zeros((64, 16), f32)
    for a in range(16):
        angle = jnp.where(((row >> 1) & 15) == a, steer_ref[a : a + 1, :], angle)
    on_row = iota((32, 32), 0) == iota((32, 32), 1)
    turns = [
        jnp.sum(jnp.where(on_row, phase_ref[c : c + 1, :], 0.0), axis=1, keepdims=True)
        for c in range(2)
    ]
    angle = angle + jnp.concatenate(turns, axis=0)
    scale = math.sqrt(0.5) / math.sqrt(steer_ref.shape[1])
    cosine, sine = jnp.cos(angle) * scale, jnp.sin(angle) * scale
    small = jnp.concatenate(
        [
            jnp.concatenate([cosine, -sine], axis=1),
            jnp.concatenate([sine, cosine], axis=1),
        ],
        axis=0,
    ).astype(bf16)
    o_at = iota((512, 128), 0)
    tall = ((o_at & 1) * 64 + (o_at >> 3) == iota((512, 128), 1)).astype(bf16)
    i_at = iota((32, 256), 1)
    broad = (((i_at >> 5) & 1) * 16 + (i_at & 15) == iota((32, 256), 0)).astype(bf16)
    spread = jnp.dot(tall, small, preferred_element_type=f32).astype(bf16)
    spread = jnp.dot(spread, broad, preferred_element_type=f32)
    o_all, i_all = iota((512, 256), 0), iota((512, 256), 1)
    same = (((o_all >> 1) & 3) == (i_all >> 6)) & ((o_all >> 8) == ((i_all >> 4) & 1))
    big_ref[...] = jnp.where(same, spread, 0.0).astype(bf16)
    o_all, i_all = iota((256, 256), 0), iota((256, 256), 1)
    order_in = (o_all & 31) * 8 + ((o_all >> 5) & 3) * 2 + (o_all >> 7)
    perm_ref[...] = (i_all == order_in).astype(bf16)

    @pl.when(is_mid)
    def _():
        foot_copy().wait_recv()

    far_sources = order_blocks([far_foot[0, f] for f in range(blocks)])

    def begin_tab():
        for d in range(1, tiles):
            peer = lax.rem(t + tiles - d, tiles)
            tab_copy(d, peer, peer).wait_recv()
        row, column = iota((3 * slots, slots * TABROWS), 0), iota((3 * slots, slots * TABROWS), 1)
        choose = column == (row & (slots - 1)) * TABROWS + row // slots
        packed_ref[g] = jnp.dot(
            choose.astype(bf16), tabs[...].reshape(slots * TABROWS, RBLOCK),
            preferred_element_type=f32,
        ).astype(bf16)
        line_tab(g, 0, inner).start()

    def relay(k):
        line_copy(k, end, 0, inner).wait_recv()
        line_copy(k, end, 1, inner).start()

    def form(u):
        @pl.when(u < POLS)
        def _():
            local_copy(u).wait()

        for j in range(3):
            @pl.when(gets(j))
            def _():
                halo_copy(u, j, True).wait_recv()

        @pl.when(is_mid & (u == 0))
        def _():
            halo_start(1)

        pieces = []
        for j in range(9):
            start = j * CBLOCK
            pieces.append(
                jnp.concatenate(
                    [ext_ref[u, 0, :, start : start + window], ext_ref[u, 1, :, start : start + window]],
                    axis=1,
                )
            )
        found = lax.dot_general(
            jnp.concatenate(pieces, axis=0), toep_ref[...], (((1,), (1,)), ((), ())),
            preferred_element_type=f32,
        ).astype(bf16)
        before = (iota((pulses, 2 * CBLOCK), 1) & (CBLOCK - 1)) < EDGE
        first = jnp.where(before & (t == 0), 0.0, found[0:pulses].astype(f32)).astype(bf16)
        for jj in range(3):
            stacked = []
            for q in range(QUARTERS):
                at = 2 * q + jj
                one = first if at == 0 else found[at * pulses : (at + 1) * pulses]
                stacked += [one[:, :CBLOCK], one[:, CBLOCK:]]
            sub_ref[:, jj * CBLOCK : (jj + 1) * CBLOCK] = jnp.dot(
                big_ref[...], jnp.concatenate(stacked, axis=0), preferred_element_type=f32
            )

        def merge(b, carry):
            totals = [None] * 4
            for c in range(2):
                by = shift_ref[c, b]
                weight = blend_ref[c, b]
                back = by < 0
                turn = jnp.where(back, by + RBLOCK, by)
                x = sub_ref[pl.ds(pl.multiple_of((c * 32 + b) * 8, 8), 8), :]
                x = jnp.concatenate([x[:, i * RBLOCK : (i + 1) * RBLOCK] for i in range(6)], axis=0)
                x = jnp.where(back, x[:40], x[8:])
                low = pltpu.roll(x, (RBLOCK - turn) & (RBLOCK - 1), 1)
                high = pltpu.roll(x, RBLOCK - 1 - turn, 1)
                lane = iota((32, RBLOCK), 1)
                low = jnp.where(lane < RBLOCK - turn, low[:32], low[8:])
                high = jnp.where(lane < RBLOCK - 1 - turn, high[:32], high[8:])
                y = (1.0 - weight) * low + weight * high
                totals = y if c == 0 else totals + y
            for i in range(4):
                merged_ref[pl.ds(pl.multiple_of(b * 8, 8), 8), i * RBLOCK : (i + 1) * RBLOCK] = (
                    totals[i * 8 : (i + 1) * 8]
                )
            return carry

        lax.fori_loop(0, 32, merge, 0, unroll=UNROLL)
        ordered = jnp.dot(
            perm_ref[...], merged_ref[...].astype(bf16), preferred_element_type=f32
        ).astype(bf16)
        for part in range(2):
            for f in range(blocks):
                at = (part * QUARTERS + f // 4) * 32
                block_ref[f, part] = ordered[at : at + 32, (f % 4) * RBLOCK : (f % 4 + 1) * RBLOCK]
        for s in range(slots):
            kid_ref[u, :, s] = block_ref[jnp.where(u < POLS, sources[s], far_sources[s])]
        spread_start(u)

    def own_line(k):
        spread_wait(k)
        line_copy(k, g, 0, inner).start()

    def forward(i):
        raw_copy(i).wait_recv()
        halo_start(POLS + i, True)

    middle = spans // 2 * RBLOCK

    def part_copy(k, half, to, place):
        span = pl.ds(half * middle, middle)
        return pltpu.make_async_remote_copy(
            src_ref=part_ref.at[k, :, :, span], dst_ref=arrived_ref.at[place, :, :, span],
            send_sem=part_send.at[k, half], recv_sem=part_recv.at[place, half],
            device_id={"pulse": to}, device_id_type=MESH,
        )

    def prepare(ref, group, beam_group, row, column, used):
        expand = (
            (iota((RBLOCK, lanes), 1) & (beams - 1)) + beam_group * beams
            == iota((RBLOCK, lanes), 0)
        ).astype(bf16)
        where_at = (iota((1, lanes), 1) // beams + 1).astype(f32)
        child = iota((32, lanes), 0).astype(f32)

        wide = jnp.dot(packed_ref[group], expand, preferred_element_type=f32)
        for at in range(slots // 4):
            pieces = []
            for slot in range(at * 4, at * 4 + 4):
                landing = wide[2 * slots + slot : 2 * slots + slot + 1, :]
                index = jnp.where(
                    (landing == where_at) & used, wide[slot : slot + 1, :], -9.0
                )
                frac = wide[slots + slot : slots + slot + 1, :]
                lower = (1.0 - frac).astype(bf16).astype(f32)
                weight = jnp.where(child == index, lower, 0.0)
                pieces.append(jnp.where(child == index + 1.0, frac, weight))
            block = jnp.concatenate(pieces, axis=0)
            at_column = pl.multiple_of(column + at * 128, 128)
            ref[row : row + lanes, pl.ds(at_column, 128)] = block.T.astype(bf16)

    def put(ref, k, half, result):
        for step in range(spans // 2):
            w = half * (spans // 2) + step
            for i in range(2):
                ref[k, i, :, w * RBLOCK : (w + 1) * RBLOCK] = result[
                    step * beams : (step + 1) * beams, i * RBLOCK : (i + 1) * RBLOCK
                ]

    side = jnp.where(g < 2, 0, 2)

    def prepare_all():
        line_tab(inner, 0, inner).wait_recv()
        line_tab(far, 0, inner).wait_recv()

        def prepare_group(group, carry):
            column = pl.multiple_of(group * depth, 128)
            prepare(left_ref, group, g, 0, column, group >= 0)

            @pl.when(group != g)
            def _():
                prepare(left_ref, group, end, lanes, column, group != end)

            return carry

        lax.fori_loop(0, 4, prepare_group, 0)

        def prepare_cross(at, carry):
            column = pl.multiple_of(at * depth, 128)
            prepare(cross_ref, side + at, far, 0, column, at >= 0)
            prepare(cross_ref, side + at, inner, lanes, column, at >= 0)
            return carry

        lax.fori_loop(0, 2, prepare_cross, 0)

    def final(k):
        line_copy(k, far, 0, inner).wait_recv()
        right = jnp.concatenate(
            [kids[:, k, i].reshape(4 * depth, RBLOCK) for i in range(2)], axis=1
        )
        for half in range(2):
            first = lanes + half * (lanes // 2)
            put(part_ref, k, half, jnp.dot(
                left_ref[first : first + lanes // 2, :], right, preferred_element_type=f32
            ).astype(bf16))
            part_copy(k, half, end, k).start()
        for half in range(2):
            first = half * (lanes // 2)
            result = jnp.dot(
                left_ref[first : first + lanes // 2, :], right, preferred_element_type=f32
            ).astype(bf16)
            for step in range(spans // 2):
                w = half * (spans // 2) + step
                for i in range(2):
                    out_ref[i, k, :, w * RBLOCK : (w + 1) * RBLOCK] = result[
                        step * beams : (step + 1) * beams, i * RBLOCK : (i + 1) * RBLOCK
                    ]

    def cross(at):
        right = jnp.concatenate(
            [kids[pl.ds(side, 2), LAST, i].reshape(2 * depth, RBLOCK) for i in range(2)], axis=1
        )
        for half in range(2):
            first = at * lanes + half * (lanes // 2)
            put(part_ref, POLS + at, half, jnp.dot(
                cross_ref[first : first + lanes // 2, :], right, preferred_element_type=f32
            ).astype(bf16))
            part_copy(POLS + at, half, inner if at else far, POLS).start()
        if at == 0:
            return
        columns = pl.ds(pl.multiple_of(side * depth, 128), 2 * depth)
        for half in range(2):
            first = half * (lanes // 2)
            put(own_ref, LAST, half, jnp.dot(
                left_ref[first : first + lanes // 2, columns], right, preferred_element_type=f32
            ))

    def last_part():
        right = jnp.concatenate(
            [kids[g, LAST, i].reshape(depth, RBLOCK) for i in range(2)], axis=1
        )
        columns = pl.ds(pl.multiple_of(g * depth, 128), depth)
        for half in range(2):
            first = lanes + half * (lanes // 2)
            put(part_ref, LAST, half, jnp.dot(
                left_ref[first : first + lanes // 2, columns], right, preferred_element_type=f32
            ).astype(bf16))
            part_copy(LAST, half, end, LAST).start()

    def mid_unit(u):
        return u // 2 + 3 * (u % 2)

    def end_unit(i):
        return jnp.where(i == 1, LAST, jnp.where(i == 0, 0, i - 1))

    def step(i, carry):
        @pl.when(is_mid & (i == 3))
        def _():
            prepare(left_ref, g, end, lanes, pl.multiple_of(g * depth, 128), g >= 0)
            spread_wait(LAST)
            last_part()
            relay(0)

        @pl.when(is_mid & (i == 4))
        def _():
            prepare_all()
            line_copy(LAST, end, 0, inner).wait_recv()
            cross(0)
            line_copy(0, inner, 0, inner).wait_recv()
            final(0)

        form(jnp.where(is_mid, mid_unit(i), end_unit(i)))

        @pl.when(i == 0)
        def _():
            begin_tab()

        @pl.when(jnp.logical_not(is_mid) & (i == 0))
        def _():
            halo_start(1)

        @pl.when(jnp.logical_not(is_mid) & (i >= 1))
        def _():
            own_line(end_unit(i - 1))

        @pl.when(is_mid & (i == 1))
        def _():
            own_line(0)
            forward(0)

        @pl.when(i == 1)
        def _():
            halo_start(2)

        @pl.when(is_mid & (i == 2))
        def _():
            line_tab(end, 0, inner).wait_recv()
            line_tab(end, 1, inner).start()
            forward(1)

        @pl.when(is_mid & (i == 4))
        def _():
            relay(1)

        return carry

    units = jnp.where(is_mid, UNITS, POLS)
    lax.fori_loop(0, units, step, 0)

    @pl.when(is_mid)
    def _():
        relay(2)
        spread_wait(1)
        spread_wait(POLS)

        def later(k, carry):
            final(k)

            @pl.when(k == 1)
            def _():
                cross(1)
                spread_wait(2)
                spread_wait(POLS + 1)

            return carry

        lax.fori_loop(1, LAST, later, 0)
        for half in range(2):
            part_copy(POLS + 1, half, inner, POLS).wait_recv()
            span = slice(half * middle, (half + 1) * middle)
            for i in range(2):
                out_ref[i, LAST, :, span] = (
                    own_ref[LAST, i, :, span] + arrived_ref[POLS, i, :, span].astype(f32)
                ).astype(bf16)
        line_tab(g, 0, inner).wait_send()
        line_tab(end, 1, inner).wait_send()
        line_copy(0, g, 0, inner).wait_send()
        for k in range(LAST):
            line_copy(k, end, 1, inner).wait_send()
        for half in range(2):
            for k in range(POLS):
                part_copy(k, half, end, k).wait_send()
            part_copy(POLS, half, far, POLS).wait_send()
            part_copy(POLS + 1, half, inner, POLS).wait_send()
        foot_copy().wait_send()
        for i in range(RAW):
            raw_copy(i).wait_send()

    @pl.when(jnp.logical_not(is_mid))
    def _():
        own_line(LAST - 1)
        prepare(left_ref, g, g, 0, 0, g >= 0)

        def product(k, carry):
            right = jnp.concatenate(
                [kids[g, k, i].reshape(depth, RBLOCK) for i in range(2)], axis=1
            )
            for half in range(2):
                first = half * (lanes // 2)
                put(own_ref, k, half, jnp.dot(
                    left_ref[first : first + lanes // 2, :depth], right,
                    preferred_element_type=f32,
                ))
            return carry

        lax.fori_loop(0, POLS, product, 0)

        def finish(k, carry):
            for half in range(2):
                part_copy(k, half, inner, k).wait_recv()
                span = slice(half * middle, (half + 1) * middle)
                for i in range(2):
                    out_ref[i, k, :, span] = (
                        own_ref[k, i, :, span] + arrived_ref[k, i, :, span].astype(f32)
                    ).astype(bf16)
            return carry

        lax.fori_loop(0, LAST, finish, 0)
        for half in range(2):
            part_copy(LAST, half, inner, LAST).wait_recv()
            part_copy(POLS, half, inner, POLS).wait_recv()
            span = slice(half * middle, (half + 1) * middle)
            for i in range(2):
                out_ref[i, LAST, :, span] = (
                    own_ref[LAST, i, :, span]
                    + arrived_ref[LAST, i, :, span].astype(f32)
                    + arrived_ref[POLS, i, :, span].astype(f32)
                ).astype(bf16)
        line_tab(g, 0, inner).wait_send()
        for k in range(POLS):
            line_copy(k, g, 0, inner).wait_send()

    for d in range(1, tiles):
        tab_copy(d, lax.rem(t + d, tiles), t).wait_send()

    def drain(u, carry):
        for d in range(1, tiles):
            spread_copy(u, d, lax.rem(t + d, tiles), t).wait_send()
        for j in range(3):
            @pl.when(sends(j))
            def _():
                halo_copy(u, j, True).wait_send()
        return carry

    lax.fori_loop(0, units, drain, 0)


def fused(
    shift, blend, foot, slot, echoes, replica, steer_phase, merge_phase, index, frac,
    tiles, beams, range_dev,
):
    slots = tiles * CAP
    lanes = range_dev // RBLOCK * beams
    bf16 = jnp.bfloat16
    f32 = jnp.float32
    pulses = echoes.shape[2]
    vmem = pl.BlockSpec(memory_space=pltpu.VMEM)
    smem = pl.BlockSpec(memory_space=pltpu.SMEM)
    dma = pltpu.SemaphoreType.DMA
    return pl.pallas_call(
        functools.partial(fused_kernel, tiles),
        out_shape=jax.ShapeDtypeStruct((2, POLS, beams, range_dev), bf16),
        in_specs=[smem] * 4 + [pl.BlockSpec(memory_space=pl.ANY)] + [vmem] * 5,
        out_specs=vmem,
        scratch_shapes=[
            pltpu.VMEM((UNITS, 2, pulses, 2 * range_dev + 2 * EDGE), bf16),
            pltpu.VMEM((2 * CBLOCK, 2 * (CBLOCK + replica.shape[1])), bf16),
            pltpu.VMEM((512, 256), bf16),
            pltpu.VMEM((256, 256), bf16),
            pltpu.VMEM((512, 3 * CBLOCK), f32),
            pltpu.VMEM((256, 4 * RBLOCK), f32),
            pltpu.VMEM((slots, 2, 32, RBLOCK), bf16),
            pltpu.VMEM((UNITS, 2, slots, 32, RBLOCK), bf16),
            pltpu.VMEM((slots, TABROWS, RBLOCK), bf16),
            pltpu.VMEM((slots, TABROWS, RBLOCK), bf16),
            pltpu.VMEM((4, POLS, 2, slots, 32, RBLOCK), bf16),
            pltpu.VMEM((slots, TABROWS, RBLOCK), bf16),
            pltpu.VMEM((4, 3 * slots, RBLOCK), bf16),
            pltpu.VMEM((2 * lanes, 4 * slots * 32), bf16),
            pltpu.VMEM((2 * lanes, 2 * slots * 32), bf16),
            pltpu.VMEM((POLS + 2, 2, beams, range_dev), bf16),
            pltpu.VMEM((POLS + 1, 2, beams, range_dev), bf16),
            pltpu.VMEM((POLS, 2, beams, range_dev), f32),
            pltpu.SMEM((1, range_dev // RBLOCK), jnp.int32),
            dma((POLS,)),
            dma((2,)),
            dma((RAW,)),
            dma((RAW,)),
            dma((UNITS, 3)),
            dma((UNITS, 3)),
            dma((UNITS + 1, tiles - 1)),
            dma((UNITS + 1, tiles - 1)),
            dma((2, POLS + 1)),
            dma((4, POLS + 1)),
            dma((POLS + 2, 2)),
            dma((POLS + 1, 2)),
        ],
        compiler_params=pltpu.CompilerParams(
            collective_id=0, has_side_effects=True, vmem_limit_bytes=40 << 20
        ),
    )(shift, blend, foot, slot, echoes, replica, steer_phase, merge_phase, index, frac)


def shards(
    echoes, replica, steer_phase, range_shift, merge_phase, merge_frac,
    footprint, row_slot, beam_index, beam_frac,
):
    pulse_count, pol_count, range_dev = echoes.shape[1:]
    rows = pulse_count * pol_count
    taps = replica.shape[1]
    final_beams = beam_index.shape[2]
    tiles = lax.axis_size("tile")
    groups = lax.axis_size("pulse")
    slot_count = tiles * CAP
    scale = 1.0 / math.sqrt(steer_phase.shape[1])
    steer_re = jnp.cos(steer_phase) * scale
    steer_im = jnp.sin(steer_phase) * scale
    steer = jnp.concatenate(
        [
            jnp.concatenate([steer_re, -steer_im], axis=1),
            jnp.concatenate([steer_im, steer_re], axis=1),
        ],
        axis=0,
    ).astype(jnp.bfloat16)
    half_root = math.sqrt(0.5)
    coef = jnp.stack(
        [
            merge_frac.reshape(-1),
            (jnp.cos(merge_phase) * half_root).reshape(-1),
            (jnp.sin(merge_phase) * half_root).reshape(-1),
        ]
    )
    beams = final_beams // groups
    if groups == 4 and slot_count == range_dev // RBLOCK:
        return fused(
            range_shift, merge_frac, footprint, row_slot, echoes.transpose(0, 2, 1, 3),
            replica, steer_phase, merge_phase, beam_index, beam_frac, tiles, beams, range_dev,
        )
    own = echoes.reshape(2, rows, range_dev)
    following = shifted(own, "tile", -1)
    before = shifted(own[:, :, range_dev - EDGE :], "tile", 1)
    after = shifted(own[:, :, :EDGE], "tile", -2)

    width = range_dev + CBLOCK
    smem = pl.BlockSpec(memory_space=pltpu.SMEM)
    vmem = pl.BlockSpec(memory_space=pltpu.VMEM)
    kids, tabs = pl.pallas_call(
        form_kernel,
        out_shape=(
            jax.ShapeDtypeStruct((8, slot_count, 32, RBLOCK), jnp.bfloat16),
            jax.ShapeDtypeStruct((slot_count, TABROWS, RBLOCK), jnp.bfloat16),
        ),
        in_specs=[smem] * 4 + [vmem] * 8,
        out_specs=(vmem, vmem),
        scratch_shapes=[
            pltpu.VMEM((2, rows, 2 * range_dev + 2 * EDGE), jnp.bfloat16),
            pltpu.VMEM((2 * CBLOCK, 2 * (CBLOCK + taps)), jnp.bfloat16),
            pltpu.VMEM((256, width), jnp.float32),
            pltpu.VMEM((256, range_dev), jnp.bfloat16),
        ],
        compiler_params=pltpu.CompilerParams(vmem_limit_bytes=56 << 20),
    )(
        range_shift, coef, footprint, row_slot,
        own, following, before, after, replica, steer, beam_index, beam_frac,
    )
    sent = jnp.concatenate(
        [kids.transpose(1, 0, 2, 3).reshape(slot_count, 256, RBLOCK), tabs], axis=1
    )
    got = lax.all_to_all(
        sent.reshape(tiles, CAP, 256 + TABROWS, RBLOCK), "tile",
        split_axis=0, concat_axis=0, tiled=True,
    ).reshape(slot_count, 256 + TABROWS, RBLOCK)
    gathered = lax.all_gather(got, "pulse", axis=0, tiled=True)
    total_slots = groups * slot_count
    image = pl.pallas_call(
        place_kernel,
        out_shape=jax.ShapeDtypeStruct((2 * pol_count, beams, range_dev), jnp.bfloat16),
        in_specs=[vmem],
        out_specs=vmem,
        scratch_shapes=[
            pltpu.VMEM((total_slots * 32, range_dev // RBLOCK * beams), jnp.bfloat16),
            pltpu.VMEM((total_slots * 32, 8 * RBLOCK), jnp.bfloat16),
        ],
        compiler_params=pltpu.CompilerParams(vmem_limit_bytes=56 << 20),
    )(gathered)
    return image.reshape(2, pol_count, beams, range_dev)


def solution(mesh):
    placed = (
        P(None, "pulse", None, "tile"),
        P(),
        P(),
        P(),
        P(),
        P(),
        P("pulse", "tile"),
        P("pulse", "tile"),
        P("pulse", "tile", None),
        P("pulse", "tile", None),
    )
    return jax.shard_map(
        shards,
        mesh=mesh,
        in_specs=placed,
        out_specs=P(None, None, "pulse", "tile"),
        check_vma=False,
    )
```
